512 devices in a mesh: narrow: 16 (over z_lo, x), wide: 32 (over y, z_hi, core).
Axes of the slice: x: 4, y: 4, z: 16 (z_hi: 4, z_lo: 4; z = z_hi * 4 + z_lo), core: 2. Of those that a mesh axis runs over, the one named last changes fastest.
Arguments:
- slices: bfloat16 [32, 4096, 4096], P(None, 'narrow', 'wide'), may hold values from -6 to 6
- mode_one: bfloat16 [4096, 512], P('narrow', 'wide'), may hold values from -6 to 6
- mode_two: bfloat16 [4096, 512], P('wide', 'narrow'), may hold values from -6 to 6
- slice_table: bfloat16 [1024, 512], replicated, may hold values from 0.0099487305 to 0.079589844
- chosen: int32 [32], replicated, may hold values from 0 to 1023
Outputs:
- new_one: bfloat16 [4096, 512], P('narrow', 'wide')
- new_two: bfloat16 [4096, 512], P('wide', 'narrow')
The draws below stay inside these ranges and needn't reach their ends.
All inputs are finite; a program needn't handle non-finite values.
Results may differ from the reference program's by a relative error of at most 0.006.
Values may be sent and summed in bfloat16 or wider, within the bound.
No kernel may reach another device: no remote copies, remote signals or barrier semaphores. Data moves between devices by JAX's collectives and lax.ppermute only.
A program may use at most 64 MiB of HBM per device.

```python
import math
import jax
import jax.numpy as jnp
from jax import lax

R = 512
BATCH = 32
KFULL = 1024
I = 4096
J = 4096


def plant(array, own_key, low, high):
    spot = [jax.random.randint(jax.random.fold_in(own_key, axis), (), 0, length) for axis, length in enumerate(array.shape)]
    main_axis = array.shape.index(max(array.shape))
    beside = spot[:main_axis] + [(spot[main_axis] + 1) % array.shape[main_axis]] + spot[main_axis + 1:]
    return array.at[tuple(spot)].set(low).at[tuple(beside)].set(high)


def level_of(key, shape, cuts, low, top_value):
    def one(dim, parts):
        heights = jax.random.uniform(jax.random.fold_in(jax.random.fold_in(key, 6), dim), (parts,), jnp.float32, low / len(cuts), top_value / len(cuts))
        return jnp.repeat(jnp.exp(heights), shape[dim] // parts).reshape((-1,) + (1,) * (len(shape) - dim - 1))

    level = one(*cuts[0])
    for cut in cuts[1:]:
        level = level * one(*cut)
    return level


def normal_values(stream_key, shape, spread, most, pieces=(), held_as=jnp.bfloat16):
    loudness = level_of(stream_key, shape, pieces, -0.22, 0.18) if pieces else 1.0
    drawn = jax.random.normal(stream_key, shape, jnp.float32) * spread * loudness
    return jnp.minimum(jnp.maximum(drawn, -most), most).astype(held_as)


def setup_inputs(seed: int = 0) -> dict:
    arg_keys = jax.random.split(jax.random.key(seed), 6)
    return {
        "slices": normal_values(arg_keys[0], (BATCH, I, J), 1.0, 6.0, ((1, 16), (2, 32))),
        "mode_one": normal_values(arg_keys[1], (I, R), 1.0, 6.0, ((0, 16), (1, 32))),
        "mode_two": normal_values(arg_keys[2], (J, R), 1.0, 6.0, ((0, 32), (1, 16))),
        "slice_table": jnp.clip(jnp.exp(jax.random.uniform(arg_keys[3], (KFULL, R), jnp.float32, math.log(0.0099487305), math.log(0.079589844))), 0.0099487305, 0.079589844).astype(jnp.bfloat16),
        "chosen": plant(jax.random.randint(arg_keys[4], (BATCH,), 0, KFULL), jax.random.fold_in(arg_keys[4], 1), 0, KFULL - 1).astype(jnp.int32),
    }


epsilon = 1e-06
step_size = 0.5

def renew(factor, gradient):
    inverse = lax.rsqrt(lax.optimization_barrier(jnp.mean(gradient * gradient, axis=1, keepdims=True)) + epsilon)
    return (factor.astype(jnp.float32) - step_size * gradient * inverse).astype(jnp.bfloat16)

def reference(slices, mode_one, mode_two, slice_table, chosen):
    slice_rows = jnp.take(slice_table, chosen.astype(jnp.int32), axis=0)
    second = mode_two.astype(jnp.float32)

    def sweep_one(total, inputs):
        target, row_scale = inputs
        scaled_two = (second * row_scale.astype(jnp.float32)[None, :]).astype(jnp.bfloat16)
        model_one = jnp.dot(mode_one, scaled_two.T, preferred_element_type=jnp.float32)
        error_one = jnp.tanh(model_one - target.astype(jnp.float32)).astype(jnp.bfloat16)
        return (total + jnp.dot(error_one, scaled_two, preferred_element_type=jnp.float32), None)
    grad_one, _ = lax.scan(sweep_one, jnp.zeros((I, R), jnp.float32), (slices, slice_rows))
    new_one = renew(mode_one, grad_one)
    first = new_one.astype(jnp.float32)

    def sweep_two(total, inputs):
        target, row_scale = inputs
        scaled_one = (first * row_scale.astype(jnp.float32)[None, :]).astype(jnp.bfloat16)
        model_two = jnp.dot(scaled_one, mode_two.T, preferred_element_type=jnp.float32)
        error_two = jnp.tanh(model_two - target.astype(jnp.float32)).astype(jnp.bfloat16)
        return (total + jnp.dot(error_two.T, scaled_one, preferred_element_type=jnp.float32), None)
    grad_two, _ = lax.scan(sweep_two, jnp.zeros((J, R), jnp.float32), (slices, slice_rows))
    new_two = renew(mode_two, grad_two)
    return (new_one, new_two)
```

```python
import jax
import jax.numpy as jnp
from jax import lax
from jax.sharding import Mesh, PartitionSpec as P

R = 512


epsilon = 1e-06
step_size = 0.5

YZ = ("y", "zh")
NARROW = ("zl", "x")
WIDE = ("y", "zh", "c")
bf16 = jnp.bfloat16
f32 = jnp.float32


def spread(block, axes, count):
    copies = jnp.broadcast_to(block[None], (count,) + block.shape)
    return lax.all_to_all(copies, axes, 0, 0, tiled=True)


def renew(rows, grad):
    inverse = lax.rsqrt(jnp.sum(grad * grad, axis=1, keepdims=True) / R + epsilon)
    return (rows.astype(f32) - step_size * grad * inverse).astype(bf16)


def body(slices, mode_one, mode_two, slice_table, chosen):
    yz, c = lax.axis_index(YZ), lax.axis_index("c")
    n, w = lax.axis_index(NARROW), lax.axis_index(WIDE)
    one_hot = (
        chosen[:, None]
        == lax.broadcasted_iota(jnp.int32, (chosen.shape[0], slice_table.shape[0]), 1)
    ).astype(bf16)
    slice_rows = jnp.dot(one_hot, slice_table, preferred_element_type=f32)
    target = slices.astype(f32)

    two_t = spread(mode_two.T, NARROW, 16).reshape(R, 128)
    full_two = two_t.T
    one_t = spread(mode_one.T, YZ, 16)
    one_t = lax.all_gather(one_t, "c", axis=0).transpose(1, 0, 2, 3).reshape(R, 256)
    full_one = one_t.T

    scaled_two = (full_two.astype(f32)[None, :, :] * slice_rows[:, None, :]).astype(bf16)
    model_one = jnp.einsum("ir,kjr->kij", full_one, scaled_two, preferred_element_type=f32)
    error_one = jnp.tanh(model_one - target).astype(bf16)
    partial_one = jnp.einsum("kij,kjr->ir", error_one, scaled_two, preferred_element_type=f32)

    pair = lax.all_gather(partial_one.astype(bf16), "c", axis=0)
    half = lax.dynamic_slice_in_dim(pair, c * 128, 128, axis=1).astype(f32)
    half = (half[0] + half[1]).astype(bf16)
    parts = lax.all_to_all(half.reshape(16, 8, R), YZ, 0, 0, tiled=True)
    grad_one = jnp.sum(parts.astype(f32), axis=0)
    own = lax.dynamic_slice_in_dim(full_one, c * 128 + yz * 8, 8, axis=0)
    new_rows = renew(own, grad_one)
    new_half = spread(new_rows, YZ, 16).reshape(128, R)
    new_full = lax.all_gather(new_half, "c", axis=0, tiled=True)
    new_one = lax.dynamic_slice_in_dim(new_full, w * 16, 16, axis=1)

    scaled_one = (new_full.astype(f32)[None, :, :] * slice_rows[:, None, :]).astype(bf16)
    model_two = jnp.einsum("kir,jr->kij", scaled_one, full_two, preferred_element_type=f32)
    error_two = jnp.tanh(model_two - target).astype(bf16)
    partial_two = jnp.einsum("kij,kir->jr", error_two, scaled_one, preferred_element_type=f32)

    parts_two = lax.all_to_all(partial_two.astype(bf16).reshape(16, 8, R), NARROW, 0, 0, tiled=True)
    grad_two = jnp.sum(parts_two.astype(f32), axis=0)
    own_two = lax.dynamic_slice_in_dim(full_two, n * 8, 8, axis=0)
    rows_two = renew(own_two, grad_two)
    blocks = rows_two.reshape(8, 16, 32).transpose(1, 0, 2)
    new_two = lax.all_to_all(blocks, NARROW, 0, 0, tiled=True).reshape(128, 32)
    return (new_one, new_two)


def solution(mesh):
    fine = Mesh(mesh.devices.reshape(4, 4, 4, 4, 2), ("zl", "x", "y", "zh", "c"))
    in_specs = (P(None, NARROW, WIDE), P(NARROW, WIDE), P(WIDE, NARROW), P(), P())
    out_specs = (P(NARROW, WIDE), P(WIDE, NARROW))
    return jax.shard_map(body, mesh=fine, in_specs=in_specs, out_specs=out_specs, check_vma=False)
```

```python
import jax
import jax.numpy as jnp
from jax import lax
from jax.experimental import pallas as pl
from jax.experimental.pallas import tpu as pltpu
from jax.sharding import Mesh, PartitionSpec as P

R = 512


epsilon = 1e-06
step_size = 0.5

YZ = ("y", "zh")
NARROW = ("zl", "x")
WIDE = ("y", "zh", "c")
bf16 = jnp.bfloat16
f32 = jnp.float32

NN = (((1,), (0,)), ((), ()))
NT = (((1,), (1,)), ((), ()))
TN = (((0,), (0,)), ((), ()))
CHUNKS = 4
BATCH = 32


def dot(a, b, dims):
    return lax.dot_general(a, b, dims, preferred_element_type=f32)


def pick(first, count, total):
    col = lax.broadcasted_iota(jnp.int32, (count, total), 1)
    row = lax.broadcasted_iota(jnp.int32, (count, total), 0)
    return (col == row + first).astype(bf16)


def fetch_kernel(t_hbm, t, sems):
    size = BATCH // CHUNKS
    copies = [
        pltpu.make_async_copy(t_hbm.at[pl.ds(q * size, size)], t.at[pl.ds(q * size, size)], sems.at[q])
        for q in range(CHUNKS)
    ]
    for copy in copies:
        copy.start()
    for copy in copies:
        copy.wait()


def errors(s, left, two, t, k):
    scaled = jnp.concatenate([two[...] * s[0:1], two[...] * s[1:2]], axis=0).astype(bf16)
    model = dot(left, scaled, NT)
    target = jnp.concatenate([t[k], t[k + 1]], axis=1).astype(f32)
    return scaled, jnp.tanh(model - target).astype(bf16)


def first_kernel(pos, s_ref, one_ref, two_ref, t, out_ref, own_ref, one_t, one, two, acc):
    for b in range(16):
        for c in range(2):
            one_t[pl.ds(32 * b + 16 * c, 16), :] = one_ref[c, b]
    one[...] = one_t[...].T
    two[...] = two_ref[...].reshape(R, 128).astype(f32).T
    acc[...] = jnp.zeros_like(acc)
    own_ref[...] = dot(pick(pos[0], 8, 256), one[...], NN)
    for k in range(0, BATCH, 2):
        scaled, error = errors(s_ref[k : k + 2, :], one[...], two, t, k)
        acc[...] += dot(error, scaled, NN)
    out_ref[...] = acc[...].astype(bf16)


def second_kernel(pos, s_ref, new_ref, two_ref, t, out_ref, block_ref, own_ref, two, acc):
    two[...] = two_ref[...].reshape(R, 128).astype(f32).T
    acc[...] = jnp.zeros_like(acc)
    block_ref[...] = dot(pick(pos[1], 16, R), new_ref[...], NT).astype(bf16)
    own_ref[...] = dot(pick(pos[2], 8, 128), two[...].astype(bf16), NN)
    for k in range(0, BATCH, 2):
        s = s_ref[k : k + 2, :]
        _, error = errors(s, new_ref[...], two, t, k)
        both = dot(error, new_ref[...], TN)
        acc[...] += both[:128] * s[0:1] + both[128:] * s[1:2]
    out_ref[...] = acc[...].astype(bf16).reshape(16, 8, R)


def pair_kernel(pos, pair_ref, out_ref):
    rows = pl.ds(pl.multiple_of(pos[3], 128), 128)
    total = pair_ref[0, rows, :].astype(f32) + pair_ref[1, rows, :].astype(f32)
    out_ref[...] = total.astype(bf16).reshape(16, 8, R)


def renew(own, parts):
    grad = jnp.sum(parts.astype(f32), axis=0)
    inverse = lax.rsqrt(jnp.sum(grad * grad, axis=1, keepdims=True) / R + epsilon)
    return own - step_size * grad * inverse


def renew_one_kernel(own_ref, parts_ref, out_ref):
    new = renew(own_ref[...], parts_ref[...]).astype(bf16)
    for b in range(16):
        out_ref[b] = new


def renew_two_kernel(own_ref, parts_ref, out_ref):
    new = renew(own_ref[...], parts_ref[...])
    for b in range(16):
        group = new[:, 128 * (b // 4) : 128 * (b // 4) + 128]
        turn = (128 - 32 * (b % 4)) % 128
        out_ref[b] = (pltpu.roll(group, turn, 1) if turn else group).astype(bf16)


def last_kernel(in_ref, out_ref):
    out_ref[...] = in_ref[...].reshape(128, 128).astype(f32).T[:32].astype(bf16)


VM = pl.BlockSpec(memory_space=pltpu.VMEM)
SM = pl.BlockSpec(memory_space=pltpu.SMEM)
HB = pl.BlockSpec(memory_space=pltpu.HBM)


def call(kernel, outs, specs, scratch=(), flops=0, nbytes=0, vmem=4):
    shapes = [jax.ShapeDtypeStruct(shape, dtype) for shape, dtype in outs]
    single = len(outs) == 1
    return pl.pallas_call(
        kernel,
        out_shape=shapes[0] if single else shapes,
        in_specs=specs,
        out_specs=VM if single else [VM] * len(outs),
        scratch_shapes=list(scratch),
        compiler_params=pltpu.CompilerParams(vmem_limit_bytes=vmem << 20),
        cost_estimate=pl.CostEstimate(flops=flops, bytes_accessed=nbytes, transcendentals=0),
    )


def spread(block, axes, count):
    copies = jnp.broadcast_to(block[None], (count,) + block.shape)
    return lax.all_to_all(copies, axes, 0, 0, tiled=True)


def body(slices, mode_one, mode_two, slice_table, chosen):
    yz, c = lax.axis_index(YZ), lax.axis_index("c")
    n, w = lax.axis_index(NARROW), lax.axis_index(WIDE)
    pos = jnp.stack([c * 128 + yz * 8, w * 16, n * 8, c * 128]).astype(jnp.int32)

    one_g = spread(mode_one.T, YZ, 16)
    two_g = spread(mode_two.T, NARROW, 16)
    one_hot = (
        chosen[:, None]
        == lax.broadcasted_iota(jnp.int32, (chosen.shape[0], slice_table.shape[0]), 1)
    ).astype(bf16)
    slice_rows = jnp.dot(one_hot, slice_table, preferred_element_type=f32)
    one_g = lax.all_gather(one_g, "c", axis=0)

    t = call(fetch_kernel, [((BATCH, 256, 128), bf16)], [HB], (pltpu.SemaphoreType.DMA((CHUNKS,)),), nbytes=1 << 21)(slices)
    half, own_one = call(
        first_kernel,
        [((256, R), bf16), ((8, R), f32)],
        [SM, VM, VM, VM, VM],
        (pltpu.VMEM((R, 256), bf16), pltpu.VMEM((256, R), bf16), pltpu.VMEM((128, R), f32), pltpu.VMEM((256, R), f32)),
        flops=1 << 31,
        vmem=16,
        nbytes=1 << 21,
    )(pos, slice_rows, one_g, two_g, t)
    pair = lax.all_gather(half, "c", axis=0)
    half = call(pair_kernel, [((16, 8, R), bf16)], [SM, VM])(pos, pair)
    parts = lax.all_to_all(half, YZ, 0, 0, tiled=True)
    copies = call(renew_one_kernel, [((16, 8, R), bf16)], [VM, VM])(own_one, parts)
    new_half = lax.all_to_all(copies, YZ, 0, 0, tiled=True).reshape(128, R)
    new_full = lax.all_gather(new_half, "c", axis=0, tiled=True)

    partial_two, new_one_t, own_two = call(
        second_kernel,
        [((16, 8, R), bf16), ((16, 256), bf16), ((8, R), f32)],
        [SM, VM, VM, VM, VM],
        (pltpu.VMEM((128, R), f32), pltpu.VMEM((128, R), f32)),
        flops=1 << 31,
        vmem=16,
        nbytes=1 << 21,
    )(pos, slice_rows, new_full, two_g, t)
    parts_two = lax.all_to_all(partial_two, NARROW, 0, 0, tiled=True)
    blocks = call(renew_two_kernel, [((16, 8, 128), bf16)], [VM, VM])(own_two, parts_two)
    blocks = lax.all_to_all(blocks, NARROW, 0, 0, tiled=True)
    new_two_t = call(last_kernel, [((32, 128), bf16)], [VM])(blocks)
    return (new_one_t.T, new_two_t.T)


def solution(mesh):
    fine = Mesh(mesh.devices.reshape(4, 4, 4, 4, 2), ("zl", "x", "y", "zh", "c"))
    in_specs = (P(None, NARROW, WIDE), P(NARROW, WIDE), P(WIDE, NARROW), P(), P())
    out_specs = (P(NARROW, WIDE), P(WIDE, NARROW))

    return jax.shard_map(body, mesh=fine, in_specs=in_specs, out_specs=out_specs, check_vma=False)
```

```python
import jax
import jax.numpy as jnp
from jax import lax
from jax.experimental import pallas as pl
from jax.experimental.pallas import tpu as pltpu
from jax.sharding import Mesh, PartitionSpec as P

R = 512


epsilon = 1e-06
step_size = 0.5

YZ = ("y", "zh")
NARROW = ("zl", "x")
WIDE = ("y", "zh", "c")
bf16 = jnp.bfloat16
f32 = jnp.float32

NN = (((1,), (0,)), ((), ()))
NT = (((1,), (1,)), ((), ()))
TN = (((0,), (0,)), ((), ()))
CHUNKS = 4
BATCH = 32


def dot(a, b, dims):
    return lax.dot_general(a, b, dims, preferred_element_type=f32)


def pick(first, count, total):
    col = lax.broadcasted_iota(jnp.int32, (count, total), 1)
    row = lax.broadcasted_iota(jnp.int32, (count, total), 0)
    return (col == row + first).astype(bf16)


def fetch_kernel(t_hbm, t, sems):
    size = BATCH // CHUNKS
    copies = [
        pltpu.make_async_copy(t_hbm.at[pl.ds(q * size, size)], t.at[pl.ds(q * size, size)], sems.at[q])
        for q in range(CHUNKS)
    ]
    for copy in copies:
        copy.start()
    for copy in copies:
        copy.wait()


def errors(s, left, two, t, k):
    scaled = jnp.concatenate([two[...] * s[0:1], two[...] * s[1:2]], axis=0).astype(bf16)
    model = dot(left, scaled, NT)
    target = jnp.concatenate([t[k], t[k + 1]], axis=1).astype(f32)
    return scaled, jnp.tanh(model - target).astype(bf16)


def first_kernel(pos, s_ref, one_ref, two_ref, t, out_ref, own_ref, one_t, one, two, acc):
    for b in range(16):
        for c in range(2):
            one_t[pl.ds(32 * b + 16 * c, 16), :] = one_ref[c, b]
    one[...] = one_t[...].T
    two[...] = two_ref[...].reshape(R, 128).astype(f32).T
    acc[...] = jnp.zeros_like(acc)
    own_ref[...] = dot(pick(pos[0], 32, 256), one[...], NN)
    for k in range(0, BATCH, 2):
        scaled, error = errors(s_ref[k : k + 2, :], one[...], two, t, k)
        acc[...] += dot(error, scaled, NN)
    out_ref[...] = acc[...].astype(bf16)


def second_kernel(pos, s_ref, new_ref, two_ref, t, out_ref, block_ref, own_ref, two, acc):
    two[...] = two_ref[...].reshape(R, 128).astype(f32).T
    acc[...] = jnp.zeros_like(acc)
    block_ref[...] = dot(pick(pos[1], 16, R), new_ref[...], NT).astype(bf16)
    own_ref[...] = dot(pick(pos[2], 8, 128), two[...].astype(bf16), NN)
    for k in range(0, BATCH, 2):
        s = s_ref[k : k + 2, :]
        _, error = errors(s, new_ref[...], two, t, k)
        both = dot(error, new_ref[...], TN)
        acc[...] += both[:128] * s[0:1] + both[128:] * s[1:2]
    out_ref[...] = acc[...].astype(bf16).reshape(16, 8, R)


def pair_kernel(pos, pair_ref, out_ref):
    rows = pl.ds(pl.multiple_of(pos[3], 128), 128)
    total = pair_ref[0, rows, :].astype(f32) + pair_ref[1, rows, :].astype(f32)
    out_ref[...] = total.astype(bf16).reshape(4, 32, R)


def sum_kernel(parts_ref, out_ref):
    total = jnp.sum(parts_ref[...].astype(f32), axis=0).astype(bf16)
    for b in range(4):
        out_ref[b] = total


def renew(own, parts):
    grad = jnp.sum(parts.astype(f32), axis=0)
    inverse = lax.rsqrt(jnp.sum(grad * grad, axis=1, keepdims=True) / R + epsilon)
    return own - step_size * grad * inverse


def renew_one_kernel(own_ref, parts_ref, out_ref):
    new = renew(own_ref[...], parts_ref[...]).astype(bf16)
    for b in range(4):
        out_ref[b] = new


def renew_two_kernel(own_ref, parts_ref, out_ref):
    new = renew(own_ref[...], parts_ref[...])
    for b in range(16):
        group = new[:, 128 * (b // 4) : 128 * (b // 4) + 128]
        turn = (128 - 32 * (b % 4)) % 128
        out_ref[b] = (pltpu.roll(group, turn, 1) if turn else group).astype(bf16)


def last_kernel(in_ref, out_ref):
    out_ref[...] = in_ref[...].reshape(128, 128).astype(f32).T[:32].astype(bf16)


VM = pl.BlockSpec(memory_space=pltpu.VMEM)
SM = pl.BlockSpec(memory_space=pltpu.SMEM)
HB = pl.BlockSpec(memory_space=pltpu.HBM)


def call(kernel, outs, specs, scratch=(), flops=0, nbytes=0, vmem=4):
    shapes = [jax.ShapeDtypeStruct(shape, dtype) for shape, dtype in outs]
    single = len(outs) == 1
    return pl.pallas_call(
        kernel,
        out_shape=shapes[0] if single else shapes,
        in_specs=specs,
        out_specs=VM if single else [VM] * len(outs),
        scratch_shapes=list(scratch),
        compiler_params=pltpu.CompilerParams(vmem_limit_bytes=vmem << 20),
        cost_estimate=pl.CostEstimate(flops=flops, bytes_accessed=nbytes, transcendentals=0),
    )


def spread(block, axes, count):
    copies = jnp.broadcast_to(block[None], (count,) + block.shape)
    return lax.all_to_all(copies, axes, 0, 0, tiled=True)


def body(slices, mode_one, mode_two, slice_table, chosen):
    y, c = lax.axis_index("y"), lax.axis_index("c")
    n, w = lax.axis_index(NARROW), lax.axis_index(WIDE)
    pos = jnp.stack([c * 128 + y * 32, w * 16, n * 8, c * 128]).astype(jnp.int32)

    one_g = spread(mode_one.T, YZ, 16)
    two_g = lax.all_gather(mode_two.T, "x", axis=0)
    two_g = lax.all_gather(two_g, "zl", axis=0).reshape(16, 32, 128)
    one_hot = (
        chosen[:, None]
        == lax.broadcasted_iota(jnp.int32, (chosen.shape[0], slice_table.shape[0]), 1)
    ).astype(bf16)
    slice_rows = jnp.dot(one_hot, slice_table, preferred_element_type=f32)
    one_g = lax.all_gather(one_g, "c", axis=0)

    t = call(fetch_kernel, [((BATCH, 256, 128), bf16)], [HB], (pltpu.SemaphoreType.DMA((CHUNKS,)),), nbytes=1 << 21)(slices)
    half, own_one = call(
        first_kernel,
        [((256, R), bf16), ((32, R), f32)],
        [SM, VM, VM, VM, VM],
        (pltpu.VMEM((R, 256), bf16), pltpu.VMEM((256, R), bf16), pltpu.VMEM((128, R), f32), pltpu.VMEM((256, R), f32)),
        flops=1 << 31,
        vmem=16,
        nbytes=1 << 21,
    )(pos, slice_rows, one_g, two_g, t)
    pair = lax.all_gather(half, "c", axis=0)
    half = call(pair_kernel, [((4, 32, R), bf16)], [SM, VM])(pos, pair)
    parts = lax.all_to_all(half, "y", 0, 0, tiled=True)
    sums = call(sum_kernel, [((4, 32, R), bf16)], [VM])(parts)
    parts = lax.all_to_all(sums, "zh", 0, 0, tiled=True)
    copies = call(renew_one_kernel, [((4, 32, R), bf16)], [VM, VM])(own_one, parts)
    new_half = lax.all_to_all(copies, "y", 0, 0, tiled=True).reshape(128, R)
    new_full = lax.all_gather(new_half, "c", axis=0, tiled=True)

    partial_two, new_one_t, own_two = call(
        second_kernel,
        [((16, 8, R), bf16), ((16, 256), bf16), ((8, R), f32)],
        [SM, VM, VM, VM, VM],
        (pltpu.VMEM((128, R), f32), pltpu.VMEM((128, R), f32)),
        flops=1 << 31,
        vmem=16,
        nbytes=1 << 21,
    )(pos, slice_rows, new_full, two_g, t)
    parts_two = lax.all_to_all(partial_two, NARROW, 0, 0, tiled=True)
    blocks = call(renew_two_kernel, [((16, 8, 128), bf16)], [VM, VM])(own_two, parts_two)
    blocks = lax.all_to_all(blocks, NARROW, 0, 0, tiled=True)
    new_two_t = call(last_kernel, [((32, 128), bf16)], [VM])(blocks)
    return (new_one_t.T, new_two_t.T)


def solution(mesh):
    fine = Mesh(mesh.devices.reshape(4, 4, 4, 4, 2), ("zl", "x", "y", "zh", "c"))
    in_specs = (P(None, NARROW, WIDE), P(NARROW, WIDE), P(WIDE, NARROW), P(), P())
    out_specs = (P(NARROW, WIDE), P(WIDE, NARROW))

    return jax.shard_map(body, mesh=fine, in_specs=in_specs, out_specs=out_specs, check_vma=False)
```

```python
import jax
import jax.numpy as jnp
from jax import lax
from jax.experimental import pallas as pl
from jax.experimental.pallas import tpu as pltpu
from jax.sharding import Mesh, PartitionSpec as P

R = 512


epsilon = 1e-06
step_size = 0.5

NARROW = ("zl", "x")
WIDE = ("y", "zh", "c")
ALL = ("zl", "x", "y", "zh", "c")
bf16 = jnp.bfloat16
f32 = jnp.float32

NN = (((1,), (0,)), ((), ()))
NT = (((1,), (1,)), ((), ()))
TN = (((0,), (0,)), ((), ()))
CHUNKS = 4
BATCH = 32


def dot(a, b, dims):
    return lax.dot_general(a, b, dims, preferred_element_type=f32)


def pick(first, count, total):
    col = lax.broadcasted_iota(jnp.int32, (count, total), 1)
    row = lax.broadcasted_iota(jnp.int32, (count, total), 0)
    return (col == row + first).astype(bf16)


def fetch_kernel(t_hbm, t, sems):
    size = BATCH // CHUNKS
    copies = [
        pltpu.make_async_copy(t_hbm.at[pl.ds(q * size, size)], t.at[pl.ds(q * size, size)], sems.at[q])
        for q in range(CHUNKS)
    ]
    for copy in copies:
        copy.start()
    for copy in copies:
        copy.wait()


def errors(s, left, two, t, k):
    scaled = jnp.concatenate([two[...] * s[0:1], two[...] * s[1:2]], axis=0).astype(bf16)
    model = dot(left, scaled, NT)
    target = jnp.concatenate([t[k], t[k + 1]], axis=1).astype(f32)
    return scaled, jnp.tanh(model - target).astype(bf16)


def first_kernel(pos, s_ref, both_ref, t, out_ref, own_ref, two_ref, one, two_t, two, acc):
    one[...] = both_ref[0].reshape(R, 256).T
    for b in range(16):
        block = both_ref[1, b, pos[4]]
        two_t[pl.ds(32 * b, 16), :] = block[:, :128]
        two_t[pl.ds(32 * b + 16, 16), :] = block[:, 128:]
    two[...] = two_t[...].astype(f32).T
    two_ref[...] = two[...]
    acc[...] = jnp.zeros_like(acc)
    own_ref[...] = dot(pick(pos[0], 32, 256), one[...], NN)
    for k in range(0, BATCH, 2):
        scaled, error = errors(s_ref[k : k + 2, :], one[...], two, t, k)
        acc[...] += dot(error, scaled, NN)
    out_ref[...] = acc[...].astype(bf16)


def second_kernel(pos, s_ref, new_ref, two, t, out_ref, block_ref, own_ref, acc):
    acc[...] = jnp.zeros_like(acc)
    block_ref[...] = dot(pick(pos[1], 16, R), new_ref[...], NT).astype(bf16)
    own_ref[...] = dot(pick(pos[2], 8, 128), two[...].astype(bf16), NN)
    for k in range(0, BATCH, 2):
        s = s_ref[k : k + 2, :]
        _, error = errors(s, new_ref[...], two, t, k)
        both = dot(error, new_ref[...], TN)
        acc[...] += both[:128] * s[0:1] + both[128:] * s[1:2]
    out_ref[...] = acc[...].astype(bf16).reshape(16, 8, R)


def pack_kernel(one_ref, two_ref, out_ref):
    out_ref[0] = one_ref[...]
    out_ref[1, :, :128] = two_ref[:16]
    out_ref[1, :, 128:] = two_ref[16:]


def pair_kernel(pos, pair_ref, out_ref):
    rows = pl.ds(pl.multiple_of(pos[3], 128), 128)
    total = pair_ref[0, rows, :].astype(f32) + pair_ref[1, rows, :].astype(f32)
    out_ref[...] = total.astype(bf16).reshape(4, 32, R)


def sum_kernel(parts_ref, out_ref):
    total = jnp.sum(parts_ref[...].astype(f32), axis=0).astype(bf16)
    for b in range(4):
        out_ref[b] = total


def renew(own, parts):
    grad = jnp.sum(parts.astype(f32), axis=0)
    inverse = lax.rsqrt(jnp.sum(grad * grad, axis=1, keepdims=True) / R + epsilon)
    return own - step_size * grad * inverse


def renew_one_kernel(own_ref, parts_ref, out_ref):
    new = renew(own_ref[...], parts_ref[...]).astype(bf16)
    for b in range(4):
        out_ref[b] = new


def renew_two_kernel(own_ref, parts_ref, out_ref):
    new = renew(own_ref[...], parts_ref[...])
    for b in range(16):
        group = new[:, 128 * (b // 4) : 128 * (b // 4) + 128]
        turn = (128 - 32 * (b % 4)) % 128
        out_ref[b] = (pltpu.roll(group, turn, 1) if turn else group).astype(bf16)


def last_kernel(in_ref, out_ref):
    out_ref[...] = in_ref[...].reshape(128, 128).astype(f32).T[:32].astype(bf16)


VM = pl.BlockSpec(memory_space=pltpu.VMEM)
SM = pl.BlockSpec(memory_space=pltpu.SMEM)
HB = pl.BlockSpec(memory_space=pltpu.HBM)


def call(kernel, outs, specs, scratch=(), flops=0, nbytes=0, vmem=4):
    shapes = [jax.ShapeDtypeStruct(shape, dtype) for shape, dtype in outs]
    single = len(outs) == 1
    return pl.pallas_call(
        kernel,
        out_shape=shapes[0] if single else shapes,
        in_specs=specs,
        out_specs=VM if single else [VM] * len(outs),
        scratch_shapes=list(scratch),
        compiler_params=pltpu.CompilerParams(vmem_limit_bytes=vmem << 20),
        cost_estimate=pl.CostEstimate(flops=flops, bytes_accessed=nbytes, transcendentals=0),
    )


def groups():
    device = lambda n, yz, c: (n * 16 + yz) * 2 + c
    first = [[device(n, yz, 0) for yz in range(16)] for n in range(16)]
    second = [[device(n, yz, 1) for n in range(16)] for yz in range(16)]
    return first + second


def body(slices, mode_one, mode_two, slice_table, chosen):
    y, c = lax.axis_index("y"), lax.axis_index("c")
    n, w = lax.axis_index(NARROW), lax.axis_index(WIDE)
    pos = jnp.stack([c * 128 + y * 32, w * 16, n * 8, c * 128, c]).astype(jnp.int32)

    mine = call(pack_kernel, [((2, 16, 256), bf16)], [VM, VM])(mode_one.T, mode_two.T)
    mine = lax.all_to_all(mine, "c", 0, 0, tiled=True)
    mine = jnp.broadcast_to(mine[None], (16, 2, 16, 256))
    both = lax.all_to_all(mine, ALL, 0, 0, axis_index_groups=groups(), tiled=True)
    one_hot = (
        chosen[:, None]
        == lax.broadcasted_iota(jnp.int32, (chosen.shape[0], slice_table.shape[0]), 1)
    ).astype(bf16)
    slice_rows = jnp.dot(one_hot, slice_table, preferred_element_type=f32)
    both = lax.all_gather(both, "c", axis=0)
    t = call(fetch_kernel, [((BATCH, 256, 128), bf16)], [HB], (pltpu.SemaphoreType.DMA((CHUNKS,)),), nbytes=1 << 21)(slices)
    half, own_one, two = call(
        first_kernel,
        [((256, R), bf16), ((32, R), f32), ((128, R), f32)],
        [SM, VM, VM, VM],
        (pltpu.VMEM((256, R), bf16), pltpu.VMEM((R, 128), bf16), pltpu.VMEM((128, R), f32), pltpu.VMEM((256, R), f32)),
        flops=1 << 31,
        vmem=16,
        nbytes=1 << 21,
    )(pos, slice_rows, both, t)
    pair = lax.all_gather(half, "c", axis=0)
    half = call(pair_kernel, [((4, 32, R), bf16)], [SM, VM])(pos, pair)
    parts = lax.all_to_all(half, "y", 0, 0, tiled=True)
    sums = call(sum_kernel, [((4, 32, R), bf16)], [VM])(parts)
    parts = lax.all_to_all(sums, "zh", 0, 0, tiled=True)
    copies = call(renew_one_kernel, [((4, 32, R), bf16)], [VM, VM])(own_one, parts)
    new_half = lax.all_to_all(copies, "y", 0, 0, tiled=True).reshape(128, R)
    new_full = lax.all_gather(new_half, "c", axis=0, tiled=True)

    partial_two, new_one_t, own_two = call(
        second_kernel,
        [((16, 8, R), bf16), ((16, 256), bf16), ((8, R), f32)],
        [SM, VM, VM, VM, VM],
        (pltpu.VMEM((128, R), f32),),
        flops=1 << 31,
        vmem=16,
        nbytes=1 << 21,
    )(pos, slice_rows, new_full, two, t)
    parts_two = lax.all_to_all(partial_two, NARROW, 0, 0, tiled=True)
    blocks = call(renew_two_kernel, [((16, 8, 128), bf16)], [VM, VM])(own_two, parts_two)
    blocks = lax.all_to_all(blocks, NARROW, 0, 0, tiled=True)
    new_two_t = call(last_kernel, [((32, 128), bf16)], [VM])(blocks)
    return (new_one_t.T, new_two_t.T)


def solution(mesh):
    fine = Mesh(mesh.devices.reshape(4, 4, 4, 4, 2), ("zl", "x", "y", "zh", "c"))
    in_specs = (P(None, NARROW, WIDE), P(NARROW, WIDE), P(WIDE, NARROW), P(), P())
    out_specs = (P(NARROW, WIDE), P(WIDE, NARROW))

    return jax.shard_map(body, mesh=fine, in_specs=in_specs, out_specs=out_specs, check_vma=False)
```

```python
import jax
import jax.numpy as jnp
from jax import lax
from jax.experimental import pallas as pl
from jax.experimental.pallas import tpu as pltpu
from jax.sharding import Mesh, PartitionSpec as P

R = 512


epsilon = 1e-06
step_size = 0.5

NARROW = ("zl", "x")
WIDE = ("y", "zh", "c")
ALL = ("zl", "x", "y", "zh", "c")
bf16 = jnp.bfloat16
f32 = jnp.float32

NN = (((1,), (0,)), ((), ()))
NT = (((1,), (1,)), ((), ()))
TN = (((0,), (0,)), ((), ()))
CHUNKS = 4
BATCH = 32


def dot(a, b, dims):
    return lax.dot_general(a, b, dims, preferred_element_type=f32)


def pick(first, count, total):
    col = lax.broadcasted_iota(jnp.int32, (count, total), 1)
    row = lax.broadcasted_iota(jnp.int32, (count, total), 0)
    return (col == row + first).astype(bf16)


def errors(s, left, two, t, k):
    scaled = jnp.concatenate([two[...] * s[0:1], two[...] * s[1:2]], axis=0).astype(bf16)
    model = dot(left, scaled, NT)
    target = jnp.concatenate([t[k], t[k + 1]], axis=1).astype(f32)
    return scaled, jnp.tanh(model - target).astype(bf16)


def fetch_kernel(t_hbm, t, sems):
    size = BATCH // CHUNKS
    copies = [
        pltpu.make_async_copy(t_hbm.at[pl.ds(q * size, size)], t.at[pl.ds(q * size, size)], sems.at[q])
        for q in range(CHUNKS)
    ]
    for copy in copies:
        copy.start()
    for copy in copies:
        copy.wait()


def first_kernel(pos, s_ref, both_ref, t, out_ref, own_ref, two_ref, one_t, one, two, acc):
    for b in range(16):
        for c in range(2):
            for h in range(2):
                one_t[pl.ds(32 * b + 16 * c, 16), pl.ds(128 * h, 128)] = both_ref[1, b, c, pl.ds(16 * h, 16), :]
    one[...] = one_t[...].T
    two[...] = both_ref[0, :, pos[4]].reshape(R, 128).astype(f32).T
    two_ref[...] = two[...]
    acc[...] = jnp.zeros_like(acc)
    own_ref[...] = dot(pick(pos[0], 32, 256), one[...], NN)
    for k in range(0, BATCH, 2):
        scaled, error = errors(s_ref[k : k + 2, :], one[...], two, t, k)
        acc[...] += dot(error, scaled, NN)
    out_ref[...] = acc[...].astype(bf16)


def second_kernel(pos, s_ref, new_ref, two, t, out_ref, block_ref, own_ref, acc):
    acc[...] = jnp.zeros_like(acc)
    block_ref[...] = dot(pick(pos[1], 16, R), new_ref[...], NT).astype(bf16)
    own_ref[...] = dot(pick(pos[2], 8, 128), two[...].astype(bf16), NN)
    for k in range(0, BATCH, 2):
        s = s_ref[k : k + 2, :]
        _, error = errors(s, new_ref[...], two, t, k)
        both = dot(error, new_ref[...], TN)
        acc[...] += both[:128] * s[0:1] + both[128:] * s[1:2]
    out_ref[...] = acc[...].astype(bf16).reshape(16, 8, R)


def spread_kernel(pos, blocks_ref, out_ref):
    kind = pos[4]
    for c in range(2):
        block = blocks_ref[c, kind]
        for b in range(16):
            out_ref[b, c] = block


def pair_kernel(pos, pair_ref, out_ref):
    rows = pl.ds(pl.multiple_of(pos[3], 128), 128)
    total = pair_ref[0, rows, :].astype(f32) + pair_ref[1, rows, :].astype(f32)
    out_ref[...] = total.astype(bf16).reshape(4, 32, R)


def sum_kernel(parts_ref, out_ref):
    total = jnp.sum(parts_ref[...].astype(f32), axis=0).astype(bf16)
    for b in range(4):
        out_ref[b] = total


def renew(own, parts):
    grad = jnp.sum(parts.astype(f32), axis=0)
    inverse = lax.rsqrt(jnp.sum(grad * grad, axis=1, keepdims=True) / R + epsilon)
    return own - step_size * grad * inverse


def renew_one_kernel(own_ref, parts_ref, out_ref):
    new = renew(own_ref[...], parts_ref[...]).astype(bf16)
    for b in range(4):
        out_ref[b] = new


def renew_two_kernel(own_ref, parts_ref, out_ref):
    new = renew(own_ref[...], parts_ref[...])
    for b in range(16):
        group = new[:, 128 * (b // 4) : 128 * (b // 4) + 128]
        turn = (128 - 32 * (b % 4)) % 128
        out_ref[b] = (pltpu.roll(group, turn, 1) if turn else group).astype(bf16)


def last_kernel(in_ref, out_ref):
    out_ref[...] = in_ref[...].reshape(128, 128).astype(f32).T[:32].astype(bf16)


VM = pl.BlockSpec(memory_space=pltpu.VMEM)
SM = pl.BlockSpec(memory_space=pltpu.SMEM)
HB = pl.BlockSpec(memory_space=pltpu.HBM)


def call(kernel, outs, specs, scratch=(), flops=0, nbytes=0, vmem=4):
    shapes = [jax.ShapeDtypeStruct(shape, dtype) for shape, dtype in outs]
    single = len(outs) == 1
    return pl.pallas_call(
        kernel,
        out_shape=shapes[0] if single else shapes,
        in_specs=specs,
        out_specs=VM if single else [VM] * len(outs),
        scratch_shapes=list(scratch),
        compiler_params=pltpu.CompilerParams(vmem_limit_bytes=vmem << 20),
        cost_estimate=pl.CostEstimate(flops=flops, bytes_accessed=nbytes, transcendentals=0),
    )


def groups():
    device = lambda n, yz, c: (n * 16 + yz) * 2 + c
    first = [[device(n, yz, 1) for yz in range(16)] for n in range(16)]
    second = [[device(n, yz, 0) for n in range(16)] for yz in range(16)]
    return first + second


def body(slices, mode_one, mode_two, slice_table, chosen):
    y, c = lax.axis_index("y"), lax.axis_index("c")
    n, w = lax.axis_index(NARROW), lax.axis_index(WIDE)
    pos = jnp.stack([c * 128 + y * 32, w * 16, n * 8, c * 128, c]).astype(jnp.int32)

    one_t = mode_one.T
    blocks = jnp.concatenate([mode_two.T, one_t[:, :128], one_t[:, 128:]], axis=0)
    blocks = lax.all_gather(blocks, "c", axis=0).reshape(2, 2, 32, 128)
    mine = call(spread_kernel, [((16, 2, 32, 128), bf16)], [SM, VM])(pos, blocks)
    both = lax.all_to_all(mine, ALL, 0, 0, axis_index_groups=groups(), tiled=True)
    both = lax.all_gather(both, "c", axis=0)
    one_hot = (
        chosen[:, None] == lax.broadcasted_iota(jnp.int32, (chosen.shape[0], slice_table.shape[0]), 1)
    ).astype(bf16)
    slice_rows = jnp.dot(one_hot, slice_table, preferred_element_type=f32)
    t = call(fetch_kernel, [((BATCH, 256, 128), bf16)], [HB], (pltpu.SemaphoreType.DMA((CHUNKS,)),), nbytes=1 << 21)(slices)
    half, own_one, two = call(
        first_kernel,
        [((256, R), bf16), ((32, R), f32), ((128, R), f32)],
        [SM, VM, VM, VM],
        (pltpu.VMEM((R, 256), bf16), pltpu.VMEM((256, R), bf16), pltpu.VMEM((128, R), f32), pltpu.VMEM((256, R), f32)),
        flops=1 << 31,
        vmem=16,
        nbytes=1 << 21,
    )(pos, slice_rows, both, t)
    pair = lax.all_gather(half, "c", axis=0)
    half = call(pair_kernel, [((4, 32, R), bf16)], [SM, VM])(pos, pair)
    parts = lax.all_to_all(half, "y", 0, 0, tiled=True)
    sums = call(sum_kernel, [((4, 32, R), bf16)], [VM])(parts)
    parts = lax.all_to_all(sums, "zh", 0, 0, tiled=True)
    copies = call(renew_one_kernel, [((4, 32, R), bf16)], [VM, VM])(own_one, parts)
    new_half = lax.all_to_all(copies, "y", 0, 0, tiled=True).reshape(128, R)
    new_full = lax.all_gather(new_half, "c", axis=0, tiled=True)

    partial_two, new_one_t, own_two = call(
        second_kernel,
        [((16, 8, R), bf16), ((16, 256), bf16), ((8, R), f32)],
        [SM, VM, VM, VM, VM],
        (pltpu.VMEM((128, R), f32),),
        flops=1 << 31,
        vmem=16,
        nbytes=1 << 21,
    )(pos, slice_rows, new_full, two, t)
    parts_two = lax.all_to_all(partial_two, NARROW, 0, 0, tiled=True)
    blocks = call(renew_two_kernel, [((16, 8, 128), bf16)], [VM, VM])(own_two, parts_two)
    blocks = lax.all_to_all(blocks, NARROW, 0, 0, tiled=True)
    new_two_t = call(last_kernel, [((32, 128), bf16)], [VM])(blocks)
    return (new_one_t.T, new_two_t.T)


def solution(mesh):
    fine = Mesh(mesh.devices.reshape(4, 4, 4, 4, 2), ("zl", "x", "y", "zh", "c"))
    in_specs = (P(None, NARROW, WIDE), P(NARROW, WIDE), P(WIDE, NARROW), P(), P())
    out_specs = (P(NARROW, WIDE), P(WIDE, NARROW))

    return jax.shard_map(body, mesh=fine, in_specs=in_specs, out_specs=out_specs, check_vma=False)
```

```python
import jax
import jax.numpy as jnp
from jax import lax
from jax.experimental import pallas as pl
from jax.experimental.pallas import tpu as pltpu
from jax.sharding import Mesh, PartitionSpec as P

R = 512


epsilon = 1e-06
step_size = 0.5

NARROW = ("zl", "x")
WIDE = ("y", "zh", "c")
ALL = ("zl", "x", "y", "zh", "c")
bf16 = jnp.bfloat16
f32 = jnp.float32

NN = (((1,), (0,)), ((), ()))
NT = (((1,), (1,)), ((), ()))
TN = (((0,), (0,)), ((), ()))
CHUNKS = 4
BATCH = 32


def dot(a, b, dims):
    return lax.dot_general(a, b, dims, preferred_element_type=f32)


def pick(first, count, total):
    col = lax.broadcasted_iota(jnp.int32, (count, total), 1)
    row = lax.broadcasted_iota(jnp.int32, (count, total), 0)
    return (col == row + first).astype(bf16)


def errors(s, left, two, t, k):
    scaled = jnp.concatenate([two[...] * s[0:1], two[...] * s[1:2]], axis=0).astype(bf16)
    model = dot(left, scaled, NT)
    target = jnp.concatenate([t[k], t[k + 1]], axis=1).astype(f32)
    return scaled, jnp.tanh(model - target).astype(bf16)


def first_kernel(
    pos, table_hbm, both_ref, t_hbm, out_ref, own_ref, two_ref, s_ref,
    t, sems, table, one_t, one, two, acc,
):
    size = BATCH // CHUNKS
    rows = pltpu.make_async_copy(table_hbm, table, sems.at[CHUNKS])
    rows.start()
    loads = [
        pltpu.make_async_copy(t_hbm.at[pl.ds(q * size, size)], t.at[pl.ds(q * size, size)], sems.at[q])
        for q in range(CHUNKS)
    ]
    for load in loads:
        load.start()
    for b in range(16):
        for c in range(2):
            for h in range(2):
                one_t[pl.ds(32 * b + 16 * c, 16), pl.ds(128 * h, 128)] = both_ref[1, b, c, pl.ds(16 * h, 16), :]
    one[...] = one_t[...].T
    two[...] = both_ref[0, :, pos[4]].reshape(R, 128).astype(f32).T
    two_ref[...] = two[...]
    acc[...] = jnp.zeros_like(acc)
    own_ref[...] = dot(pick(pos[0], 32, 256), one[...], NN)
    row = lax.broadcasted_iota(jnp.int32, (BATCH, 128), 0)
    lane = lax.broadcasted_iota(jnp.int32, (BATCH, 128), 1)
    index = jnp.zeros((BATCH, 128), jnp.int32)
    for k in range(BATCH):
        index = jnp.where(row == k, pos[5 + k], index)
    hot = [(lane + first == index).astype(f32) for first in range(0, table.shape[0], 128)]
    rows.wait()
    s_ref[...] = dot(jnp.concatenate(hot, axis=1).astype(bf16), table[...], NN)
    for k in range(0, BATCH, 2):
        if k % size == 0:
            loads[k // size].wait()
        scaled, error = errors(s_ref[k : k + 2, :], one[...], two, t, k)
        acc[...] += dot(error, scaled, NN)
    out_ref[...] = acc[...].astype(bf16)


def second_kernel(pos, s_ref, new_ref, two, t, out_ref, block_ref, own_ref, acc):
    acc[...] = jnp.zeros_like(acc)
    block_ref[...] = dot(pick(pos[1], 16, R), new_ref[...], NT).astype(bf16)
    own_ref[...] = dot(pick(pos[2], 8, 128), two[...].astype(bf16), NN)
    for k in range(0, BATCH, 2):
        s = s_ref[k : k + 2, :]
        _, error = errors(s, new_ref[...], two, t, k)
        both = dot(error, new_ref[...], TN)
        acc[...] += both[:128] * s[0:1] + both[128:] * s[1:2]
    out_ref[...] = acc[...].astype(bf16).reshape(16, 8, R)


def spread_kernel(pos, blocks_ref, out_ref):
    kind = pos[4]
    for c in range(2):
        block = blocks_ref[c, kind]
        for b in range(16):
            out_ref[b, c] = block


def pair_kernel(pos, pair_ref, out_ref):
    rows = pl.ds(pl.multiple_of(pos[3], 128), 128)
    total = pair_ref[0, rows, :].astype(f32) + pair_ref[1, rows, :].astype(f32)
    out_ref[...] = total.astype(bf16).reshape(4, 32, R)


def sum_kernel(parts_ref, out_ref):
    total = jnp.sum(parts_ref[...].astype(f32), axis=0).astype(bf16)
    for b in range(4):
        out_ref[b] = total


def renew(own, parts):
    grad = jnp.sum(parts.astype(f32), axis=0)
    inverse = lax.rsqrt(jnp.sum(grad * grad, axis=1, keepdims=True) / R + epsilon)
    return own - step_size * grad * inverse


def renew_one_kernel(own_ref, parts_ref, out_ref):
    new = renew(own_ref[...], parts_ref[...]).astype(bf16)
    for b in range(4):
        out_ref[b] = new


def renew_two_kernel(own_ref, parts_ref, out_ref):
    new = renew(own_ref[...], parts_ref[...])
    for b in range(16):
        group = new[:, 128 * (b // 4) : 128 * (b // 4) + 128]
        turn = (128 - 32 * (b % 4)) % 128
        out_ref[b] = (pltpu.roll(group, turn, 1) if turn else group).astype(bf16)


def last_kernel(in_ref, out_ref):
    out_ref[...] = in_ref[...].reshape(128, 128).astype(f32).T[:32].astype(bf16)


VM = pl.BlockSpec(memory_space=pltpu.VMEM)
SM = pl.BlockSpec(memory_space=pltpu.SMEM)
HB = pl.BlockSpec(memory_space=pltpu.HBM)


def call(kernel, outs, specs, scratch=(), flops=0, nbytes=0, vmem=4):
    shapes = [jax.ShapeDtypeStruct(shape, dtype) for shape, dtype in outs]
    single = len(outs) == 1
    return pl.pallas_call(
        kernel,
        out_shape=shapes[0] if single else shapes,
        in_specs=specs,
        out_specs=VM if single else [VM] * len(outs),
        scratch_shapes=list(scratch),
        compiler_params=pltpu.CompilerParams(vmem_limit_bytes=vmem << 20),
        cost_estimate=pl.CostEstimate(flops=flops, bytes_accessed=nbytes, transcendentals=0),
    )


def groups():
    device = lambda n, yz, c: (n * 16 + yz) * 2 + c
    first = [[device(n, yz, 1) for yz in range(16)] for n in range(16)]
    second = [[device(n, yz, 0) for n in range(16)] for yz in range(16)]
    return first + second


def body(slices, mode_one, mode_two, slice_table, chosen):
    y, c = lax.axis_index("y"), lax.axis_index("c")
    n, w = lax.axis_index(NARROW), lax.axis_index(WIDE)
    pos = jnp.stack([c * 128 + y * 32, w * 16, n * 8, c * 128, c]).astype(jnp.int32)
    pos = jnp.concatenate([pos, chosen])

    one_t = mode_one.T
    blocks = jnp.concatenate([mode_two.T, one_t[:, :128], one_t[:, 128:]], axis=0)
    blocks = lax.all_gather(blocks, "c", axis=0).reshape(2, 2, 32, 128)
    mine = call(spread_kernel, [((16, 2, 32, 128), bf16)], [SM, VM])(pos, blocks)
    both = lax.all_to_all(mine, ALL, 0, 0, axis_index_groups=groups(), tiled=True)
    both = lax.all_gather(both, "c", axis=0)
    half, own_one, two, slice_rows = call(
        first_kernel,
        [((256, R), bf16), ((32, R), f32), ((128, R), f32), ((BATCH, R), f32)],
        [SM, HB, VM, HB],
        (pltpu.VMEM((BATCH, 256, 128), bf16), pltpu.SemaphoreType.DMA((CHUNKS + 1,)), pltpu.VMEM((1024, R), bf16), pltpu.VMEM((R, 256), bf16), pltpu.VMEM((256, R), bf16), pltpu.VMEM((128, R), f32), pltpu.VMEM((256, R), f32)),
        flops=1 << 31,
        vmem=52,
        nbytes=1 << 21,
    )(pos, slice_table, both, slices)
    pair = lax.all_gather(half, "c", axis=0)
    half = call(pair_kernel, [((4, 32, R), bf16)], [SM, VM])(pos, pair)
    parts = lax.all_to_all(half, "y", 0, 0, tiled=True)
    sums = call(sum_kernel, [((4, 32, R), bf16)], [VM])(parts)
    parts = lax.all_to_all(sums, "zh", 0, 0, tiled=True)
    copies = call(renew_one_kernel, [((4, 32, R), bf16)], [VM, VM])(own_one, parts)
    new_half = lax.all_to_all(copies, "y", 0, 0, tiled=True).reshape(128, R)
    new_full = lax.all_gather(new_half, "c", axis=0, tiled=True)

    partial_two, new_one_t, own_two = call(
        second_kernel,
        [((16, 8, R), bf16), ((16, 256), bf16), ((8, R), f32)],
        [SM, VM, VM, VM, VM],
        (pltpu.VMEM((128, R), f32),),
        flops=1 << 31,
        vmem=16,
        nbytes=1 << 21,
    )(pos, slice_rows, new_full, two, slices)
    parts_two = lax.all_to_all(partial_two, NARROW, 0, 0, tiled=True)
    blocks = call(renew_two_kernel, [((16, 8, 128), bf16)], [VM, VM])(own_two, parts_two)
    blocks = lax.all_to_all(blocks, NARROW, 0, 0, tiled=True)
    new_two_t = call(last_kernel, [((32, 128), bf16)], [VM])(blocks)
    return (new_one_t.T, new_two_t.T)


def solution(mesh):
    fine = Mesh(mesh.devices.reshape(4, 4, 4, 4, 2), ("zl", "x", "y", "zh", "c"))
    in_specs = (P(None, NARROW, WIDE), P(NARROW, WIDE), P(WIDE, NARROW), P(), P())
    out_specs = (P(NARROW, WIDE), P(WIDE, NARROW))

    return jax.shard_map(body, mesh=fine, in_specs=in_specs, out_specs=out_specs, check_vma=False)
```

```python
import jax
import jax.numpy as jnp
from jax import lax
from jax.experimental import pallas as pl
from jax.experimental.pallas import tpu as pltpu
from jax.sharding import Mesh, PartitionSpec as P

R = 512


epsilon = 1e-06
step_size = 0.5

NARROW = ("zl", "x")
WIDE = ("y", "zh", "c")
ALL = ("zl", "x", "y", "zh", "c")
bf16 = jnp.bfloat16
f32 = jnp.float32

NN = (((1,), (0,)), ((), ()))
NT = (((1,), (1,)), ((), ()))
TN = (((0,), (0,)), ((), ()))
CHUNKS = 4
BATCH = 32
STEP = 8


def dot(a, b, dims):
    return lax.dot_general(a, b, dims, preferred_element_type=f32)


def pick(first, count, total):
    col = lax.broadcasted_iota(jnp.int32, (count, total), 1)
    row = lax.broadcasted_iota(jnp.int32, (count, total), 0)
    return (col == row + first).astype(bf16)


def errors(s, left, two, t, k):
    scaled = jnp.concatenate([two[...] * s[q : q + 1] for q in range(STEP)], axis=0).astype(bf16)
    model = dot(left, scaled, NT)
    target = jnp.concatenate([t[k + q] for q in range(STEP)], axis=1).astype(f32)
    return scaled, jnp.tanh(model - target).astype(bf16)


def fetch_kernel(t_hbm, t, sems):
    size = BATCH // CHUNKS
    copies = [
        pltpu.make_async_copy(t_hbm.at[pl.ds(q * size, size)], t.at[pl.ds(q * size, size)], sems.at[q])
        for q in range(CHUNKS)
    ]
    for copy in copies:
        copy.start()
    for copy in copies:
        copy.wait()


def first_kernel(pos, s_ref, both_ref, t, out_ref, own_ref, two_ref, one_t, one, two, acc):
    for b in range(16):
        for c in range(2):
            for h in range(4):
                rows, lanes = pl.ds(32 * b + 16 * c + 8 * (h // 2), 8), pl.ds(128 * (h % 2), 128)
                one_t[rows, lanes] = both_ref[1, b, c, h]
    one[...] = one_t[...].T
    two[...] = both_ref[0, :, pos[3]].reshape(R, 128).astype(f32).T
    two_ref[...] = two[...]
    acc[...] = jnp.zeros_like(acc)
    own_ref[...] = dot(pick(pos[0], 32, 256), one[...], NN)
    for k in range(0, BATCH, STEP):
        scaled, error = errors(s_ref[k : k + STEP, :], one[...], two, t, k)
        acc[...] += dot(error, scaled, NN)
    out_ref[...] = acc[...].astype(bf16).reshape(8, 32, R)


def second_kernel(pos, s_ref, new_ref, two, t, out_ref, block_ref, own_ref, acc):
    acc[...] = jnp.zeros_like(acc)
    block_ref[...] = dot(pick(pos[1], 16, R), new_ref[...], NT).astype(bf16)
    own_ref[...] = dot(pick(pos[2], 8, 128), two[...].astype(bf16), NN)
    for k in range(0, BATCH, STEP):
        s = s_ref[k : k + STEP, :]
        _, error = errors(s, new_ref[...], two, t, k)
        both = dot(error, new_ref[...], TN)
        total = acc[...]
        for q in range(STEP):
            total = total + both[128 * q : 128 * q + 128] * s[q : q + 1]
        acc[...] = total
    out_ref[...] = acc[...].astype(bf16).reshape(16, 8, R)


def sum_kernel(parts_ref, out_ref):
    total = jnp.sum(parts_ref[...].astype(f32), axis=0).astype(bf16)
    for b in range(4):
        out_ref[b] = total


def renew(own, parts):
    grad = jnp.sum(parts.astype(f32), axis=0)
    inverse = lax.rsqrt(jnp.sum(grad * grad, axis=1, keepdims=True) / R + epsilon)
    return own - step_size * grad * inverse


def renew_one_kernel(own_ref, parts_ref, out_ref):
    new = renew(own_ref[...], parts_ref[...]).astype(bf16)
    for b in range(8):
        out_ref[b] = new


def renew_two_kernel(own_ref, parts_ref, out_ref):
    new = renew(own_ref[...], parts_ref[...])
    for b in range(16):
        group = new[:, 128 * (b // 4) : 128 * (b // 4) + 128]
        turn = (128 - 32 * (b % 4)) % 128
        out_ref[b] = (pltpu.roll(group, turn, 1) if turn else group).astype(bf16)


def last_kernel(in_ref, out_ref):
    out_ref[...] = in_ref[...].reshape(128, 128).astype(f32).T[:32].astype(bf16)


VM = pl.BlockSpec(memory_space=pltpu.VMEM)
SM = pl.BlockSpec(memory_space=pltpu.SMEM)
HB = pl.BlockSpec(memory_space=pltpu.HBM)


def call(kernel, outs, specs, scratch=(), flops=0, nbytes=0, vmem=4):
    shapes = [jax.ShapeDtypeStruct(shape, dtype) for shape, dtype in outs]
    single = len(outs) == 1
    return pl.pallas_call(
        kernel,
        out_shape=shapes[0] if single else shapes,
        in_specs=specs,
        out_specs=VM if single else [VM] * len(outs),
        scratch_shapes=list(scratch),
        compiler_params=pltpu.CompilerParams(vmem_limit_bytes=vmem << 20),
        cost_estimate=pl.CostEstimate(flops=flops, bytes_accessed=nbytes, transcendentals=0),
    )


def groups():
    device = lambda n, yz, c: (n * 16 + yz) * 2 + c
    first = [[device(n, yz, 1) for yz in range(16)] for n in range(16)]
    second = [[device(n, yz, 0) for n in range(16)] for yz in range(16)]
    return first + second


def body(slices, mode_one, mode_two, slice_table, chosen):
    y, c = lax.axis_index("y"), lax.axis_index("c")
    n, w = lax.axis_index(NARROW), lax.axis_index(WIDE)
    pos = jnp.stack([(y * 2 + c) * 32, w * 16, n * 8, c]).astype(jnp.int32)

    tiles = mode_one.T.reshape(2, 8, 2, 128).transpose(0, 2, 1, 3).reshape(4, 8, 128)
    blocks = jnp.concatenate([mode_two.T.reshape(4, 8, 128), tiles], axis=0)
    blocks = lax.all_gather(blocks, "c", axis=0).reshape(2, 2, 4, 8, 128)
    mine = lax.dynamic_index_in_dim(blocks, c, axis=1, keepdims=False)
    mine = jnp.broadcast_to(mine[None], (16, 2, 4, 8, 128))
    both = lax.all_to_all(mine, ALL, 0, 0, axis_index_groups=groups(), tiled=True)
    both = lax.all_gather(both, "c", axis=0)
    one_hot = (
        chosen[:, None] == lax.broadcasted_iota(jnp.int32, (chosen.shape[0], slice_table.shape[0]), 1)
    ).astype(bf16)
    slice_rows = jnp.dot(one_hot, slice_table, preferred_element_type=f32)
    t = call(fetch_kernel, [((BATCH, 256, 128), bf16)], [HB], (pltpu.SemaphoreType.DMA((CHUNKS,)),), nbytes=1 << 21)(slices)
    partial_one, own_one, two = call(
        first_kernel,
        [((8, 32, R), bf16), ((32, R), f32), ((128, R), f32)],
        [SM, VM, VM, VM],
        (pltpu.VMEM((R, 256), bf16), pltpu.VMEM((256, R), bf16), pltpu.VMEM((128, R), f32), pltpu.VMEM((256, R), f32)),
        flops=1 << 31,
        vmem=16,
        nbytes=1 << 21,
    )(pos, slice_rows, both, t)
    parts = lax.all_to_all(partial_one, ("y", "c"), 0, 0, tiled=True)
    sums = call(sum_kernel, [((4, 32, R), bf16)], [VM])(parts)
    parts = lax.all_to_all(sums, "zh", 0, 0, tiled=True)
    copies = call(renew_one_kernel, [((8, 32, R), bf16)], [VM, VM])(own_one, parts)
    new_full = lax.all_to_all(copies, ("y", "c"), 0, 0, tiled=True).reshape(256, R)

    partial_two, new_one_t, own_two = call(
        second_kernel,
        [((16, 8, R), bf16), ((16, 256), bf16), ((8, R), f32)],
        [SM, VM, VM, VM, VM],
        (pltpu.VMEM((128, R), f32),),
        flops=1 << 31,
        vmem=16,
        nbytes=1 << 21,
    )(pos, slice_rows, new_full, two, t)
    parts_two = lax.all_to_all(partial_two, NARROW, 0, 0, tiled=True)
    blocks = call(renew_two_kernel, [((16, 8, 128), bf16)], [VM, VM])(own_two, parts_two)
    blocks = lax.all_to_all(blocks, NARROW, 0, 0, tiled=True)
    new_two_t = call(last_kernel, [((32, 128), bf16)], [VM])(blocks)
    return (new_one_t.T, new_two_t.T)


def solution(mesh):
    fine = Mesh(mesh.devices.reshape(4, 4, 4, 4, 2), ("zl", "x", "y", "zh", "c"))
    in_specs = (P(None, NARROW, WIDE), P(NARROW, WIDE), P(WIDE, NARROW), P(), P())
    out_specs = (P(NARROW, WIDE), P(WIDE, NARROW))

    return jax.shard_map(body, mesh=fine, in_specs=in_specs, out_specs=out_specs, check_vma=False)
```

```python
import jax
import jax.numpy as jnp
from jax import lax
from jax.experimental import pallas as pl
from jax.experimental.pallas import tpu as pltpu
from jax.sharding import Mesh, PartitionSpec as P

R = 512


epsilon = 1e-06
step_size = 0.5

NARROW = ("zl", "x")
WIDE = ("y", "zh", "c")
ALL = ("zl", "x", "y", "zh", "c")
bf16 = jnp.bfloat16
f32 = jnp.float32

NN = (((1,), (0,)), ((), ()))
NT = (((1,), (1,)), ((), ()))
TN = (((0,), (0,)), ((), ()))
CHUNKS = 4
BATCH = 32
STEP = 8


def dot(a, b, dims):
    return lax.dot_general(a, b, dims, preferred_element_type=f32)


def pick(first, count, total):
    col = lax.broadcasted_iota(jnp.int32, (count, total), 1)
    row = lax.broadcasted_iota(jnp.int32, (count, total), 0)
    return (col == row + first).astype(bf16)


def errors(s, left, two, t, k):
    scaled = jnp.concatenate([two[...] * s[q : q + 1] for q in range(STEP)], axis=0).astype(bf16)
    model = dot(left, scaled, NT)
    target = jnp.concatenate([t[k + q] for q in range(STEP)], axis=1).astype(f32)
    return scaled, jnp.tanh(model - target).astype(bf16)


def fetch_kernel(t_hbm, t, sems):
    size = BATCH // CHUNKS
    copies = [
        pltpu.make_async_copy(t_hbm.at[pl.ds(q * size, size)], t.at[pl.ds(q * size, size)], sems.at[q])
        for q in range(CHUNKS)
    ]
    for copy in copies:
        copy.start()
    for copy in copies:
        copy.wait()


def first_kernel(pos, s_ref, both_ref, t, out_ref, own_ref, two_ref, one_t, two_t, one, two, acc):
    for b in range(16):
        for c in range(2):
            for h in range(4):
                rows, lanes = pl.ds(32 * b + 16 * c + 8 * (h // 2), 8), pl.ds(128 * (h % 2), 128)
                one_t[rows, lanes] = both_ref[1, b, c, h]
    one[...] = one_t[...].T
    for p in range(16):
        two_t[pl.ds(p % 4 * 128 + p // 4 * 32, 32), :] = both_ref[0, p, pos[3]].reshape(32, 128)
    two[...] = two_t[...].astype(f32).T
    two_ref[...] = two[...]
    acc[...] = jnp.zeros_like(acc)
    own_ref[...] = dot(pick(pos[0], 32, 256), one[...], NN)
    for k in range(0, BATCH, STEP):
        scaled, error = errors(s_ref[k : k + STEP, :], one[...], two, t, k)
        acc[...] += dot(error, scaled, NN)
    out_ref[...] = acc[...].astype(bf16).reshape(8, 32, R)


def second_kernel(pos, s_ref, new_ref, two, t, out_ref, block_ref, own_ref, acc):
    acc[...] = jnp.zeros_like(acc)
    block_ref[...] = dot(pick(pos[1], 16, R), new_ref[...], NT).astype(bf16)
    own_ref[...] = dot(pick(pos[2], 8, 128), two[...].astype(bf16), NN)
    for k in range(0, BATCH, STEP):
        s = s_ref[k : k + STEP, :]
        _, error = errors(s, new_ref[...], two, t, k)
        both = dot(error, new_ref[...], TN)
        total = acc[...]
        for q in range(STEP):
            total = total + both[128 * q : 128 * q + 128] * s[q : q + 1]
        acc[...] = total
    out_ref[...] = acc[...].astype(bf16).reshape(16, 8, R)


def sum_kernel(parts_ref, out_ref):
    total = jnp.sum(parts_ref[...].astype(f32), axis=0).astype(bf16)
    for b in range(4):
        out_ref[b] = total


def renew(own, parts):
    grad = jnp.sum(parts.astype(f32), axis=0)
    inverse = lax.rsqrt(jnp.sum(grad * grad, axis=1, keepdims=True) / R + epsilon)
    return own - step_size * grad * inverse


def renew_one_kernel(own_ref, parts_ref, out_ref):
    new = renew(own_ref[...], parts_ref[...]).astype(bf16)
    for b in range(8):
        out_ref[b] = new


def renew_two_kernel(own_ref, parts_ref, out_ref):
    new = renew(own_ref[...], parts_ref[...])
    for p in range(16):
        b = p % 4 * 4 + p // 4
        group = new[:, 128 * (b // 4) : 128 * (b // 4) + 128]
        turn = (128 - 32 * (b % 4)) % 128
        out_ref[p] = (pltpu.roll(group, turn, 1) if turn else group).astype(bf16)


def last_kernel(in_ref, out_ref):
    out_ref[...] = in_ref[...].reshape(128, 128).astype(f32).T[:32].astype(bf16)


VM = pl.BlockSpec(memory_space=pltpu.VMEM)
SM = pl.BlockSpec(memory_space=pltpu.SMEM)
HB = pl.BlockSpec(memory_space=pltpu.HBM)


def call(kernel, outs, specs, scratch=(), flops=0, nbytes=0, vmem=4):
    shapes = [jax.ShapeDtypeStruct(shape, dtype) for shape, dtype in outs]
    single = len(outs) == 1
    return pl.pallas_call(
        kernel,
        out_shape=shapes[0] if single else shapes,
        in_specs=specs,
        out_specs=VM if single else [VM] * len(outs),
        scratch_shapes=list(scratch),
        compiler_params=pltpu.CompilerParams(vmem_limit_bytes=vmem << 20),
        cost_estimate=pl.CostEstimate(flops=flops, bytes_accessed=nbytes, transcendentals=0),
    )


def groups():
    device = lambda n, yz, c: (n * 16 + yz) * 2 + c
    first = [[device(n, yz, 1) for yz in range(16)] for n in range(16)]
    second = [[device(p % 4 * 4 + p // 4, yz, 0) for p in range(16)] for yz in range(16)]
    return first + second


def body(slices, mode_one, mode_two, slice_table, chosen):
    y, c = lax.axis_index("y"), lax.axis_index("c")
    m, w = lax.axis_index(("x", "zl")), lax.axis_index(WIDE)
    pos = jnp.stack([(c * 4 + y) * 32, w * 16, m * 8, c]).astype(jnp.int32)

    tiles = mode_one.T.reshape(2, 8, 2, 128).transpose(0, 2, 1, 3).reshape(4, 8, 128)
    blocks = jnp.concatenate([mode_two.T.reshape(4, 8, 128), tiles], axis=0)
    blocks = lax.all_gather(blocks, "c", axis=0).reshape(2, 2, 4, 8, 128)
    mine = lax.dynamic_index_in_dim(blocks, c, axis=1, keepdims=False)
    mine = jnp.broadcast_to(mine[None], (16, 2, 4, 8, 128))
    both = lax.all_to_all(mine, ALL, 0, 0, axis_index_groups=groups(), tiled=True)
    both = lax.all_gather(both, "c", axis=0)
    one_hot = (
        chosen[:, None] == lax.broadcasted_iota(jnp.int32, (chosen.shape[0], slice_table.shape[0]), 1)
    ).astype(bf16)
    slice_rows = jnp.dot(one_hot, slice_table, preferred_element_type=f32)
    t = call(fetch_kernel, [((BATCH, 256, 128), bf16)], [HB], (pltpu.SemaphoreType.DMA((CHUNKS,)),), nbytes=1 << 21)(slices)
    partial_one, own_one, two = call(
        first_kernel,
        [((8, 32, R), bf16), ((32, R), f32), ((128, R), f32)],
        [SM, VM, VM, VM],
        (pltpu.VMEM((R, 256), bf16), pltpu.VMEM((R, 128), bf16), pltpu.VMEM((256, R), bf16), pltpu.VMEM((128, R), f32), pltpu.VMEM((256, R), f32)),
        flops=1 << 31,
        vmem=16,
        nbytes=1 << 21,
    )(pos, slice_rows, both, t)
    parts = lax.all_to_all(partial_one, ("c", "y"), 0, 0, tiled=True)
    sums = call(sum_kernel, [((4, 32, R), bf16)], [VM])(parts)
    parts = lax.all_to_all(sums, "zh", 0, 0, tiled=True)
    copies = call(renew_one_kernel, [((8, 32, R), bf16)], [VM, VM])(own_one, parts)
    new_full = lax.all_to_all(copies, ("c", "y"), 0, 0, tiled=True).reshape(256, R)

    partial_two, new_one_t, own_two = call(
        second_kernel,
        [((16, 8, R), bf16), ((16, 256), bf16), ((8, R), f32)],
        [SM, VM, VM, VM, VM],
        (pltpu.VMEM((128, R), f32),),
        flops=1 << 31,
        vmem=16,
        nbytes=1 << 21,
    )(pos, slice_rows, new_full, two, t)
    parts_two = lax.all_to_all(partial_two, ("x", "zl"), 0, 0, tiled=True)
    blocks = call(renew_two_kernel, [((16, 8, 128), bf16)], [VM, VM])(own_two, parts_two)
    blocks = lax.all_to_all(blocks, ("x", "zl"), 0, 0, tiled=True)
    new_two_t = call(last_kernel, [((32, 128), bf16)], [VM])(blocks)
    return (new_one_t.T, new_two_t.T)


def solution(mesh):
    fine = Mesh(mesh.devices.reshape(4, 4, 4, 4, 2), ("zl", "x", "y", "zh", "c"))
    in_specs = (P(None, NARROW, WIDE), P(NARROW, WIDE), P(WIDE, NARROW), P(), P())
    out_specs = (P(NARROW, WIDE), P(WIDE, NARROW))

    return jax.shard_map(body, mesh=fine, in_specs=in_specs, out_specs=out_specs, check_vma=False)
```

```python
import jax
import jax.numpy as jnp
from jax import lax
from jax.experimental import pallas as pl
from jax.experimental.pallas import tpu as pltpu
from jax.sharding import Mesh, PartitionSpec as P

R = 512


epsilon = 1e-06
step_size = 0.5

NARROW = ("zl", "x")
WIDE = ("y", "zh", "c")
ALL = ("zl", "x", "y", "zh", "c")
bf16 = jnp.bfloat16
f32 = jnp.float32

NN = (((1,), (0,)), ((), ()))
NT = (((1,), (1,)), ((), ()))
TN = (((0,), (0,)), ((), ()))
CHUNKS = 4
BATCH = 32
STEP = 8


def dot(a, b, dims):
    return lax.dot_general(a, b, dims, preferred_element_type=f32)


def pick(first, count, total):
    col = lax.broadcasted_iota(jnp.int32, (count, total), 1)
    row = lax.broadcasted_iota(jnp.int32, (count, total), 0)
    return (col == row + first).astype(bf16)


def errors(s, left, two, t, k):
    scaled = jnp.concatenate([two[...] * s[q : q + 1] for q in range(STEP)], axis=0).astype(bf16)
    model = dot(left, scaled, NT)
    target = jnp.concatenate([t[k + q] for q in range(STEP)], axis=1).astype(f32)
    return scaled, jnp.tanh(model - target).astype(bf16)


def fetch_kernel(t_hbm, t, sems):
    size = BATCH // CHUNKS
    copies = [
        pltpu.make_async_copy(t_hbm.at[pl.ds(q * size, size)], t.at[pl.ds(q * size, size)], sems.at[q])
        for q in range(CHUNKS)
    ]
    for copy in copies:
        copy.start()
    for copy in copies:
        copy.wait()


def first_kernel(pos, s_ref, both_ref, t, out_ref, own_ref, two_ref, one_t, two_t, one, two, acc):
    for b in range(16):
        for c in range(2):
            for h in range(4):
                rows, lanes = pl.ds(32 * b + 16 * c + 8 * (h // 2), 8), pl.ds(128 * (h % 2), 128)
                one_t[rows, lanes] = both_ref[1, b, c, h]
    one[...] = one_t[...].T
    for p in range(16):
        two_t[pl.ds(p % 4 * 128 + p // 4 * 32, 32), :] = both_ref[0, p, pos[3]].reshape(32, 128)
    two[...] = two_t[...].astype(f32).T
    two_ref[...] = two[...]
    acc[...] = jnp.zeros_like(acc)
    own_ref[...] = dot(pick(pos[0], 32, 256), one[...], NN)
    for k in range(0, BATCH, STEP):
        scaled, error = errors(s_ref[k : k + STEP, :], one[...], two, t, k)
        acc[...] += dot(error, scaled, NN)
    out_ref[...] = acc[...].astype(bf16).reshape(8, 32, R)


def second_kernel(pos, s_ref, new_ref, two, t, out_ref, block_ref, own_ref, acc):
    acc[...] = jnp.zeros_like(acc)
    block_ref[...] = dot(pick(pos[1], 16, R), new_ref[...], NT).astype(bf16)
    own_ref[...] = dot(pick(pos[2], 8, 128), two[...].astype(bf16), NN)
    for k in range(0, BATCH, STEP):
        s = s_ref[k : k + STEP, :]
        _, error = errors(s, new_ref[...], two, t, k)
        both = dot(error, new_ref[...], TN)
        total = acc[...]
        for q in range(STEP):
            total = total + both[128 * q : 128 * q + 128] * s[q : q + 1]
        acc[...] = total
    out_ref[...] = acc[...].astype(bf16).reshape(16, 8, R)


def sum_kernel(parts_ref, out_ref):
    out_ref[...] = jnp.sum(parts_ref[...].astype(f32), axis=0).astype(bf16)


def renew(own, parts):
    grad = jnp.sum(parts.astype(f32), axis=0)
    inverse = lax.rsqrt(jnp.sum(grad * grad, axis=1, keepdims=True) / R + epsilon)
    return own - step_size * grad * inverse


def renew_one_kernel(own_ref, parts_ref, out_ref):
    new = renew(own_ref[...], parts_ref[...]).astype(bf16)
    for b in range(8):
        out_ref[b] = new


def renew_two_kernel(own_ref, parts_ref, out_ref):
    new = renew(own_ref[...], parts_ref[...])
    for p in range(16):
        b = p % 4 * 4 + p // 4
        group = new[:, 128 * (b // 4) : 128 * (b // 4) + 128]
        turn = (128 - 32 * (b % 4)) % 128
        out_ref[p] = (pltpu.roll(group, turn, 1) if turn else group).astype(bf16)


def last_kernel(in_ref, out_ref):
    out_ref[...] = in_ref[...].reshape(128, 128).astype(f32).T[:32].astype(bf16)


VM = pl.BlockSpec(memory_space=pltpu.VMEM)
SM = pl.BlockSpec(memory_space=pltpu.SMEM)
HB = pl.BlockSpec(memory_space=pltpu.HBM)


def call(kernel, outs, specs, scratch=(), flops=0, nbytes=0, vmem=4):
    shapes = [jax.ShapeDtypeStruct(shape, dtype) for shape, dtype in outs]
    single = len(outs) == 1
    return pl.pallas_call(
        kernel,
        out_shape=shapes[0] if single else shapes,
        in_specs=specs,
        out_specs=VM if single else [VM] * len(outs),
        scratch_shapes=list(scratch),
        compiler_params=pltpu.CompilerParams(vmem_limit_bytes=vmem << 20),
        cost_estimate=pl.CostEstimate(flops=flops, bytes_accessed=nbytes, transcendentals=0),
    )


def groups():
    device = lambda n, yz, c: (n * 16 + yz) * 2 + c
    first = [[device(n, yz, 1) for yz in range(16)] for n in range(16)]
    second = [[device(p % 4 * 4 + p // 4, yz, 0) for p in range(16)] for yz in range(16)]
    return first + second


def body(slices, mode_one, mode_two, slice_table, chosen):
    y, c = lax.axis_index("y"), lax.axis_index("c")
    m, w = lax.axis_index(("x", "zl")), lax.axis_index(WIDE)
    pos = jnp.stack([(c * 4 + y) * 32, w * 16, m * 8, c]).astype(jnp.int32)

    tiles = mode_one.T.reshape(2, 8, 2, 128).transpose(0, 2, 1, 3).reshape(4, 8, 128)
    blocks = jnp.concatenate([mode_two.T.reshape(4, 8, 128), tiles], axis=0)
    blocks = lax.all_gather(blocks, "c", axis=0).reshape(2, 2, 4, 8, 128)
    mine = lax.dynamic_index_in_dim(blocks, c, axis=1, keepdims=False)
    mine = jnp.broadcast_to(mine[None], (16, 2, 4, 8, 128))
    both = lax.all_to_all(mine, ALL, 0, 0, axis_index_groups=groups(), tiled=True)
    both = lax.all_gather(both, "c", axis=0)
    one_hot = (
        chosen[:, None] == lax.broadcasted_iota(jnp.int32, (chosen.shape[0], slice_table.shape[0]), 1)
    ).astype(bf16)
    slice_rows = jnp.dot(one_hot, slice_table, preferred_element_type=f32)
    t = call(fetch_kernel, [((BATCH, 256, 128), bf16)], [HB], (pltpu.SemaphoreType.DMA((CHUNKS,)),), nbytes=1 << 21)(slices)
    partial_one, own_one, two = call(
        first_kernel,
        [((8, 32, R), bf16), ((32, R), f32), ((128, R), f32)],
        [SM, VM, VM, VM],
        (pltpu.VMEM((R, 256), bf16), pltpu.VMEM((R, 128), bf16), pltpu.VMEM((256, R), bf16), pltpu.VMEM((128, R), f32), pltpu.VMEM((256, R), f32)),
        flops=1 << 31,
        vmem=16,
        nbytes=1 << 21,
    )(pos, slice_rows, both, t)
    parts = lax.all_to_all(partial_one, ("c", "y"), 0, 0, tiled=True)
    add = call(sum_kernel, [((32, R), bf16)], [VM])
    parts = lax.all_gather(add(parts), "zh", axis=0, axis_index_groups=[[0, 1], [2, 3]])
    parts = lax.all_gather(add(parts), "zh", axis=0, axis_index_groups=[[1, 2], [3, 0]])
    copies = call(renew_one_kernel, [((8, 32, R), bf16)], [VM, VM])(own_one, parts)
    new_full = lax.all_to_all(copies, ("c", "y"), 0, 0, tiled=True).reshape(256, R)

    partial_two, new_one_t, own_two = call(
        second_kernel,
        [((16, 8, R), bf16), ((16, 256), bf16), ((8, R), f32)],
        [SM, VM, VM, VM, VM],
        (pltpu.VMEM((128, R), f32),),
        flops=1 << 31,
        vmem=16,
        nbytes=1 << 21,
    )(pos, slice_rows, new_full, two, t)
    parts_two = lax.all_to_all(partial_two, ("x", "zl"), 0, 0, tiled=True)
    blocks = call(renew_two_kernel, [((16, 8, 128), bf16)], [VM, VM])(own_two, parts_two)
    blocks = lax.all_to_all(blocks, ("x", "zl"), 0, 0, tiled=True)
    new_two_t = call(last_kernel, [((32, 128), bf16)], [VM])(blocks)
    return (new_one_t.T, new_two_t.T)


def solution(mesh):
    fine = Mesh(mesh.devices.reshape(4, 4, 4, 4, 2), ("zl", "x", "y", "zh", "c"))
    in_specs = (P(None, NARROW, WIDE), P(NARROW, WIDE), P(WIDE, NARROW), P(), P())
    out_specs = (P(NARROW, WIDE), P(WIDE, NARROW))

    return jax.shard_map(body, mesh=fine, in_specs=in_specs, out_specs=out_specs, check_vma=False)
```

```python
import jax
import jax.numpy as jnp
from jax import lax
from jax.experimental import pallas as pl
from jax.experimental.pallas import tpu as pltpu
from jax.sharding import Mesh, PartitionSpec as P

R = 512


epsilon = 1e-06
step_size = 0.5

NARROW = ("zl", "x")
WIDE = ("y", "zh", "c")
ALL = ("zl", "x", "y", "zh", "c")
bf16 = jnp.bfloat16
f32 = jnp.float32

NN = (((1,), (0,)), ((), ()))
NT = (((1,), (1,)), ((), ()))
TN = (((0,), (0,)), ((), ()))
CHUNKS = 4
BATCH = 32
STEP = 8


def far_first(p):
    return p // 4 * 4 + (0, 2, 1, 3)[p % 4]


def dot(a, b, dims):
    return lax.dot_general(a, b, dims, preferred_element_type=f32)


def pick(first, count, total):
    col = lax.broadcasted_iota(jnp.int32, (count, total), 1)
    row = lax.broadcasted_iota(jnp.int32, (count, total), 0)
    return (col == row + first).astype(bf16)


def errors(s, left, two, t, k):
    scaled = jnp.concatenate([two[...] * s[q : q + 1] for q in range(STEP)], axis=0).astype(bf16)
    model = dot(left, scaled, NT)
    target = jnp.concatenate([t[k + q] for q in range(STEP)], axis=1).astype(f32)
    return scaled, jnp.tanh(model - target).astype(bf16)


def fetch_kernel(t_hbm, t, sems):
    size = BATCH // CHUNKS
    copies = [
        pltpu.make_async_copy(t_hbm.at[pl.ds(q * size, size)], t.at[pl.ds(q * size, size)], sems.at[q])
        for q in range(CHUNKS)
    ]
    for copy in copies:
        copy.start()
    for copy in copies:
        copy.wait()


def first_kernel(pos, s_ref, both_ref, t, out_ref, own_ref, two_ref, one_t, two_t, one, two, acc):
    for b in range(16):
        for c in range(2):
            for h in range(4):
                rows, lanes = pl.ds(32 * b + 16 * c + 8 * (h // 2), 8), pl.ds(128 * (h % 2), 128)
                one_t[rows, lanes] = both_ref[1, far_first(b), c, h]
    one[...] = one_t[...].T
    for p in range(16):
        two_t[pl.ds(p % 4 * 128 + p // 4 * 32, 32), :] = both_ref[0, p, pos[3]].reshape(32, 128)
    two[...] = two_t[...].astype(f32).T
    two_ref[...] = two[...]
    acc[...] = jnp.zeros_like(acc)
    own_ref[...] = dot(pick(pos[0], 32, 256), one[...], NN)
    for k in range(0, BATCH, STEP):
        scaled, error = errors(s_ref[k : k + STEP, :], one[...], two, t, k)
        acc[...] += dot(error, scaled, NN)
    out_ref[...] = acc[...].astype(bf16).reshape(8, 32, R)


def second_kernel(pos, s_ref, new_ref, two, t, out_ref, block_ref, own_ref, acc):
    acc[...] = jnp.zeros_like(acc)
    block_ref[...] = dot(pick(pos[1], 16, R), new_ref[...], NT).astype(bf16)
    own_ref[...] = dot(pick(pos[2], 8, 128), two[...].astype(bf16), NN)
    for k in range(0, BATCH, STEP):
        s = s_ref[k : k + STEP, :]
        _, error = errors(s, new_ref[...], two, t, k)
        both = dot(error, new_ref[...], TN)
        total = acc[...]
        for q in range(STEP):
            total = total + both[128 * q : 128 * q + 128] * s[q : q + 1]
        acc[...] = total
    out_ref[...] = acc[...].astype(bf16).reshape(16, 8, R)


def sum_kernel(parts_ref, out_ref):
    out_ref[...] = jnp.sum(parts_ref[...].astype(f32), axis=0).astype(bf16)


def renew(own, parts):
    grad = jnp.sum(parts.astype(f32), axis=0)
    inverse = lax.rsqrt(jnp.sum(grad * grad, axis=1, keepdims=True) / R + epsilon)
    return own - step_size * grad * inverse


def renew_one_kernel(own_ref, parts_ref, out_ref):
    new = renew(own_ref[...], parts_ref[...]).astype(bf16)
    for b in range(8):
        out_ref[b] = new


def renew_two_kernel(own_ref, parts_ref, out_ref):
    new = renew(own_ref[...], parts_ref[...])
    for p in range(16):
        b = p % 4 * 4 + p // 4
        group = new[:, 128 * (b // 4) : 128 * (b // 4) + 128]
        turn = (128 - 32 * (b % 4)) % 128
        out_ref[p] = (pltpu.roll(group, turn, 1) if turn else group).astype(bf16)


def last_kernel(in_ref, out_ref):
    out_ref[...] = in_ref[...].reshape(128, 128).astype(f32).T[:32].astype(bf16)


VM = pl.BlockSpec(memory_space=pltpu.VMEM)
SM = pl.BlockSpec(memory_space=pltpu.SMEM)
HB = pl.BlockSpec(memory_space=pltpu.HBM)


def call(kernel, outs, specs, scratch=(), flops=0, nbytes=0, vmem=4):
    shapes = [jax.ShapeDtypeStruct(shape, dtype) for shape, dtype in outs]
    single = len(outs) == 1
    return pl.pallas_call(
        kernel,
        out_shape=shapes[0] if single else shapes,
        in_specs=specs,
        out_specs=VM if single else [VM] * len(outs),
        scratch_shapes=list(scratch),
        compiler_params=pltpu.CompilerParams(vmem_limit_bytes=vmem << 20),
        cost_estimate=pl.CostEstimate(flops=flops, bytes_accessed=nbytes, transcendentals=0),
    )


def groups():
    device = lambda n, yz, c: (n * 16 + yz) * 2 + c
    first = [[device(n, far_first(p), 1) for p in range(16)] for n in range(16)]
    second = [[device(p % 4 * 4 + p // 4, yz, 0) for p in range(16)] for yz in range(16)]
    return first + second


def body(slices, mode_one, mode_two, slice_table, chosen):
    y, c = lax.axis_index("y"), lax.axis_index("c")
    m, w = lax.axis_index(("x", "zl")), lax.axis_index(WIDE)
    pos = jnp.stack([(c * 4 + y) * 32, w * 16, m * 8, c]).astype(jnp.int32)

    tiles = mode_one.T.reshape(2, 8, 2, 128).transpose(0, 2, 1, 3).reshape(4, 8, 128)
    blocks = jnp.concatenate([mode_two.T.reshape(4, 8, 128), tiles], axis=0)
    blocks = lax.all_gather(blocks, "c", axis=0).reshape(2, 2, 4, 8, 128)
    mine = lax.dynamic_index_in_dim(blocks, c, axis=1, keepdims=False)
    mine = jnp.broadcast_to(mine[None], (16, 2, 4, 8, 128))
    both = lax.all_to_all(mine, ALL, 0, 0, axis_index_groups=groups(), tiled=True)
    both = lax.all_gather(both, "c", axis=0)
    one_hot = (
        chosen[:, None] == lax.broadcasted_iota(jnp.int32, (chosen.shape[0], slice_table.shape[0]), 1)
    ).astype(bf16)
    slice_rows = jnp.dot(one_hot, slice_table, preferred_element_type=f32)
    t = call(fetch_kernel, [((BATCH, 256, 128), bf16)], [HB], (pltpu.SemaphoreType.DMA((CHUNKS,)),), nbytes=1 << 21)(slices)
    partial_one, own_one, two = call(
        first_kernel,
        [((8, 32, R), bf16), ((32, R), f32), ((128, R), f32)],
        [SM, VM, VM, VM],
        (pltpu.VMEM((R, 256), bf16), pltpu.VMEM((R, 128), bf16), pltpu.VMEM((256, R), bf16), pltpu.VMEM((128, R), f32), pltpu.VMEM((256, R), f32)),
        flops=1 << 31,
        vmem=16,
        nbytes=1 << 21,
    )(pos, slice_rows, both, t)
    parts = lax.all_to_all(partial_one, ("c", "y"), 0, 0, tiled=True)
    add = call(sum_kernel, [((32, R), bf16)], [VM])
    parts = lax.all_gather(add(parts), "zh", axis=0, axis_index_groups=[[0, 1], [2, 3]])
    parts = lax.all_gather(add(parts), "zh", axis=0, axis_index_groups=[[1, 2], [3, 0]])
    copies = call(renew_one_kernel, [((8, 32, R), bf16)], [VM, VM])(own_one, parts)
    new_full = lax.all_to_all(copies, ("c", "y"), 0, 0, tiled=True).reshape(256, R)

    partial_two, new_one_t, own_two = call(
        second_kernel,
        [((16, 8, R), bf16), ((16, 256), bf16), ((8, R), f32)],
        [SM, VM, VM, VM, VM],
        (pltpu.VMEM((128, R), f32),),
        flops=1 << 31,
        vmem=16,
        nbytes=1 << 21,
    )(pos, slice_rows, new_full, two, t)
    parts_two = lax.all_to_all(partial_two, ("x", "zl"), 0, 0, tiled=True)
    blocks = call(renew_two_kernel, [((16, 8, 128), bf16)], [VM, VM])(own_two, parts_two)
    blocks = lax.all_to_all(blocks, ("x", "zl"), 0, 0, tiled=True)
    new_two_t = call(last_kernel, [((32, 128), bf16)], [VM])(blocks)
    return (new_one_t.T, new_two_t.T)


def solution(mesh):
    fine = Mesh(mesh.devices.reshape(4, 4, 4, 4, 2), ("zl", "x", "y", "zh", "c"))
    in_specs = (P(None, NARROW, WIDE), P(NARROW, WIDE), P(WIDE, NARROW), P(), P())
    out_specs = (P(NARROW, WIDE), P(WIDE, NARROW))

    return jax.shard_map(body, mesh=fine, in_specs=in_specs, out_specs=out_specs, check_vma=False)
```

```python
import jax
import jax.numpy as jnp
from jax import lax
from jax.experimental import pallas as pl
from jax.experimental.pallas import tpu as pltpu
from jax.sharding import Mesh, PartitionSpec as P

R = 512


epsilon = 1e-06
step_size = 0.5

NARROW = ("zl", "x")
WIDE = ("y", "zh", "c")
ALL = ("zl", "x", "y", "zh", "c")
bf16 = jnp.bfloat16
f32 = jnp.float32

NN = (((1,), (0,)), ((), ()))
NT = (((1,), (1,)), ((), ()))
TN = (((0,), (0,)), ((), ()))
CHUNKS = 4
BATCH = 32
STEP = 8


def far_first(p):
    return p // 4 * 4 + (0, 2, 1, 3)[p % 4]


def dot(a, b, dims):
    return lax.dot_general(a, b, dims, preferred_element_type=f32)


def pick(first, count, total):
    col = lax.broadcasted_iota(jnp.int32, (count, total), 1)
    row = lax.broadcasted_iota(jnp.int32, (count, total), 0)
    return (col == row + first).astype(bf16)


def errors(s, left, two, t, k):
    scaled = jnp.concatenate([two[...] * s[q : q + 1] for q in range(STEP)], axis=0).astype(bf16)
    model = dot(left, scaled, NT)
    target = jnp.concatenate([t[k + q] for q in range(STEP)], axis=1).astype(f32)
    return scaled, jnp.tanh(model - target).astype(bf16)


def fetch_kernel(t_hbm, t, sems):
    size = BATCH // CHUNKS
    copies = [
        pltpu.make_async_copy(t_hbm.at[pl.ds(q * size, size)], t.at[pl.ds(q * size, size)], sems.at[q])
        for q in range(CHUNKS)
    ]
    for copy in copies:
        copy.start()
    for copy in copies:
        copy.wait()


def first_kernel(pos, s_ref, both_ref, t, out_ref, own_ref, two_ref, one_t, two_t, one, two, acc):
    for b in range(16):
        for c in range(2):
            for h in range(4):
                rows, lanes = pl.ds(32 * b + 16 * c + 8 * (h // 2), 8), pl.ds(128 * (h % 2), 128)
                one_t[rows, lanes] = both_ref[1, far_first(b), c, h]
    one[...] = one_t[...].T
    for p in range(16):
        two_t[pl.ds(p % 4 * 128 + p // 4 * 32, 32), :] = both_ref[0, p, pos[3]].reshape(32, 128)
    two[...] = two_t[...].astype(f32).T
    two_ref[...] = two[...]
    acc[...] = jnp.zeros_like(acc)
    own_ref[...] = dot(pick(pos[0], 32, 256), one[...], NN)
    for k in range(0, BATCH, STEP):
        scaled, error = errors(s_ref[k : k + STEP, :], one[...], two, t, k)
        acc[...] += dot(error, scaled, NN)
    total = acc[...].astype(bf16).reshape(8, 32, R)
    out_ref[pl.ds(4 * pos[4], 4)] = total[:4]
    out_ref[pl.ds(4 * (1 - pos[4]), 4)] = total[4:]


def second_kernel(pos, s_ref, halves_ref, two, t, out_ref, block_ref, own_ref, new_ref, acc):
    new_ref[:128] = halves_ref[pl.ds(4 * pos[4], 4)].reshape(128, R)
    new_ref[128:] = halves_ref[pl.ds(4 * (1 - pos[4]), 4)].reshape(128, R)
    acc[...] = jnp.zeros_like(acc)
    block_ref[...] = dot(pick(pos[1], 16, R), new_ref[...], NT).astype(bf16)
    own_ref[...] = dot(pick(pos[2], 8, 128), two[...].astype(bf16), NN)
    for k in range(0, BATCH, STEP):
        s = s_ref[k : k + STEP, :]
        _, error = errors(s, new_ref[...], two, t, k)
        both = dot(error, new_ref[...], TN)
        total = acc[...]
        for q in range(STEP):
            total = total + both[128 * q : 128 * q + 128] * s[q : q + 1]
        acc[...] = total
    out_ref[...] = acc[...].astype(bf16).reshape(16, 8, R)


def sum_kernel(parts_ref, out_ref):
    out_ref[...] = jnp.sum(parts_ref[...].astype(f32), axis=0).astype(bf16)


def renew(own, parts):
    grad = jnp.sum(parts.astype(f32), axis=0)
    inverse = lax.rsqrt(jnp.sum(grad * grad, axis=1, keepdims=True) / R + epsilon)
    return own - step_size * grad * inverse


def renew_one_kernel(own_ref, parts_ref, out_ref):
    new = renew(own_ref[...], parts_ref[...]).astype(bf16)
    for b in range(8):
        out_ref[b] = new


def renew_two_kernel(own_ref, parts_ref, out_ref):
    new = renew(own_ref[...], parts_ref[...])
    for p in range(16):
        b = p % 4 * 4 + p // 4
        group = new[:, 128 * (b // 4) : 128 * (b // 4) + 128]
        turn = (128 - 32 * (b % 4)) % 128
        out_ref[p] = (pltpu.roll(group, turn, 1) if turn else group).astype(bf16)


def last_kernel(in_ref, out_ref):
    out_ref[...] = in_ref[...].reshape(128, 128).astype(f32).T[:32].astype(bf16)


VM = pl.BlockSpec(memory_space=pltpu.VMEM)
SM = pl.BlockSpec(memory_space=pltpu.SMEM)
HB = pl.BlockSpec(memory_space=pltpu.HBM)


def call(kernel, outs, specs, scratch=(), flops=0, nbytes=0, vmem=4):
    shapes = [jax.ShapeDtypeStruct(shape, dtype) for shape, dtype in outs]
    single = len(outs) == 1
    return pl.pallas_call(
        kernel,
        out_shape=shapes[0] if single else shapes,
        in_specs=specs,
        out_specs=VM if single else [VM] * len(outs),
        scratch_shapes=list(scratch),
        compiler_params=pltpu.CompilerParams(vmem_limit_bytes=vmem << 20),
        cost_estimate=pl.CostEstimate(flops=flops, bytes_accessed=nbytes, transcendentals=0),
    )


def groups():
    device = lambda n, yz, c: (n * 16 + yz) * 2 + c
    first = [[device(n, far_first(p), 1) for p in range(16)] for n in range(16)]
    second = [[device(p % 4 * 4 + p // 4, yz, 0) for p in range(16)] for yz in range(16)]
    return first + second


def pairs(first):
    return [[z % 4 * 2 + c, (z + 1) % 4 * 2 + 1 - c] for z in (first, first + 2) for c in range(2)]


def body(slices, mode_one, mode_two, slice_table, chosen):
    y, c = lax.axis_index("y"), lax.axis_index("c")
    odd = lax.axis_index("zh") & 1
    m, w = lax.axis_index(("x", "zl")), lax.axis_index(WIDE)
    pos = jnp.stack([((c ^ odd) * 4 + y) * 32, w * 16, m * 8, c, odd]).astype(jnp.int32)

    tiles = mode_one.T.reshape(2, 8, 2, 128).transpose(0, 2, 1, 3).reshape(4, 8, 128)
    blocks = jnp.concatenate([mode_two.T.reshape(4, 8, 128), tiles], axis=0)
    blocks = lax.all_gather(blocks, "c", axis=0).reshape(2, 2, 4, 8, 128)
    mine = lax.dynamic_index_in_dim(blocks, c, axis=1, keepdims=False)
    mine = jnp.broadcast_to(mine[None], (16, 2, 4, 8, 128))
    both = lax.all_to_all(mine, ALL, 0, 0, axis_index_groups=groups(), tiled=True)
    both = lax.all_gather(both, "c", axis=0)
    one_hot = (
        chosen[:, None] == lax.broadcasted_iota(jnp.int32, (chosen.shape[0], slice_table.shape[0]), 1)
    ).astype(bf16)
    slice_rows = jnp.dot(one_hot, slice_table, preferred_element_type=f32)
    t = call(fetch_kernel, [((BATCH, 256, 128), bf16)], [HB], (pltpu.SemaphoreType.DMA((CHUNKS,)),), nbytes=1 << 21)(slices)
    partial_one, own_one, two = call(
        first_kernel,
        [((8, 32, R), bf16), ((32, R), f32), ((128, R), f32)],
        [SM, VM, VM, VM],
        (pltpu.VMEM((R, 256), bf16), pltpu.VMEM((R, 128), bf16), pltpu.VMEM((256, R), bf16), pltpu.VMEM((128, R), f32), pltpu.VMEM((256, R), f32)),
        flops=1 << 31,
        vmem=16,
        nbytes=1 << 21,
    )(pos, slice_rows, both, t)
    parts = lax.all_to_all(partial_one, ("c", "y"), 0, 0, tiled=True)
    add = call(sum_kernel, [((32, R), bf16)], [VM])
    parts = lax.all_gather(add(parts), ("zh", "c"), axis=0, axis_index_groups=pairs(0))
    parts = lax.all_gather(add(parts), ("zh", "c"), axis=0, axis_index_groups=pairs(1))
    copies = call(renew_one_kernel, [((8, 32, R), bf16)], [VM, VM])(own_one, parts)
    new_full = lax.all_to_all(copies, ("c", "y"), 0, 0, tiled=True)

    partial_two, new_one_t, own_two = call(
        second_kernel,
        [((16, 8, R), bf16), ((16, 256), bf16), ((8, R), f32)],
        [SM, VM, VM, VM, VM],
        (pltpu.VMEM((256, R), bf16), pltpu.VMEM((128, R), f32)),
        flops=1 << 31,
        vmem=16,
        nbytes=1 << 21,
    )(pos, slice_rows, new_full, two, t)
    parts_two = lax.all_to_all(partial_two, ("x", "zl"), 0, 0, tiled=True)
    blocks = call(renew_two_kernel, [((16, 8, 128), bf16)], [VM, VM])(own_two, parts_two)
    blocks = lax.all_to_all(blocks, ("x", "zl"), 0, 0, tiled=True)
    new_two_t = call(last_kernel, [((32, 128), bf16)], [VM])(blocks)
    return (new_one_t.T, new_two_t.T)


def solution(mesh):
    fine = Mesh(mesh.devices.reshape(4, 4, 4, 4, 2), ("zl", "x", "y", "zh", "c"))
    in_specs = (P(None, NARROW, WIDE), P(NARROW, WIDE), P(WIDE, NARROW), P(), P())
    out_specs = (P(NARROW, WIDE), P(WIDE, NARROW))

    return jax.shard_map(body, mesh=fine, in_specs=in_specs, out_specs=out_specs, check_vma=False)
```

```python
import jax
import jax.numpy as jnp
from jax import lax
from jax.experimental import pallas as pl
from jax.experimental.pallas import tpu as pltpu
from jax.sharding import Mesh, PartitionSpec as P

R = 512


epsilon = 1e-06
step_size = 0.5

NARROW = ("zl", "x")
WIDE = ("y", "zh", "c")
ALL = ("zl", "x", "y", "zh", "c")
bf16 = jnp.bfloat16
f32 = jnp.float32

NN = (((1,), (0,)), ((), ()))
NT = (((1,), (1,)), ((), ()))
TN = (((0,), (0,)), ((), ()))
CHUNKS = 4
BATCH = 32
STEP = 8
WIDE_STEP = 16


def far_first(p):
    return p // 4 * 4 + (0, 2, 1, 3)[p % 4]


def dot(a, b, dims):
    return lax.dot_general(a, b, dims, preferred_element_type=f32)


def pick(first, count, total):
    col = lax.broadcasted_iota(jnp.int32, (count, total), 1)
    row = lax.broadcasted_iota(jnp.int32, (count, total), 0)
    return (col == row + first).astype(bf16)


def errors(s, left, two, t, k):
    count = s.shape[0]
    scaled = jnp.concatenate([two[...] * s[q : q + 1] for q in range(count)], axis=0).astype(bf16)
    model = dot(left, scaled, NT)
    target = jnp.concatenate([t[k + q] for q in range(count)], axis=1).astype(f32)
    return scaled, jnp.tanh(model - target).astype(bf16)


def fetch_kernel(t_hbm, t, sems):
    size = BATCH // CHUNKS
    copies = [
        pltpu.make_async_copy(t_hbm.at[pl.ds(q * size, size)], t.at[pl.ds(q * size, size)], sems.at[q])
        for q in range(CHUNKS)
    ]
    for copy in copies:
        copy.start()
    for copy in copies:
        copy.wait()


def first_kernel(pos, s_ref, both_ref, t, out_ref, own_ref, two_ref, one_t, two_t, one, two, acc):
    for b in range(16):
        for c in range(2):
            for h in range(4):
                rows, lanes = pl.ds(32 * b + 16 * c + 8 * (h // 2), 8), pl.ds(128 * (h % 2), 128)
                one_t[rows, lanes] = both_ref[1, far_first(b), c, h]
    one[...] = one_t[...].T
    for p in range(16):
        two_t[pl.ds(p % 4 * 128 + p // 4 * 32, 32), :] = both_ref[0, p, pos[3]].reshape(32, 128)
    two[...] = two_t[...].astype(f32).T
    two_ref[...] = two[...]
    acc[...] = jnp.zeros_like(acc)
    own_ref[...] = dot(pick(pos[0], 32, 256), one[...], NN)
    for k in range(0, BATCH, STEP):
        scaled, error = errors(s_ref[k : k + STEP, :], one[...], two, t, k)
        acc[...] += dot(error, scaled, NN)
    total = acc[...].astype(bf16).reshape(8, 32, R)
    out_ref[pl.ds(4 * pos[4], 4)] = total[:4]
    out_ref[pl.ds(4 * (1 - pos[4]), 4)] = total[4:]


def second_kernel(pos, s_ref, halves_ref, two, t, out_ref, block_ref, own_ref, new_ref, acc):
    new_ref[:128] = halves_ref[pl.ds(4 * pos[4], 4)].reshape(128, R)
    new_ref[128:] = halves_ref[pl.ds(4 * (1 - pos[4]), 4)].reshape(128, R)
    acc[...] = jnp.zeros_like(acc)
    block_ref[...] = dot(pick(pos[1], 16, R), new_ref[...], NT).astype(bf16)
    own_ref[...] = dot(pick(pos[2], 8, 128), two[...].astype(bf16), NN)
    for k in range(0, BATCH, WIDE_STEP):
        s = s_ref[k : k + WIDE_STEP, :]
        _, error = errors(s, new_ref[...], two, t, k)
        both = dot(error, new_ref[...], TN)
        total = acc[...]
        for q in range(WIDE_STEP):
            total = total + both[128 * q : 128 * q + 128] * s[q : q + 1]
        acc[...] = total
    out_ref[...] = acc[...].astype(bf16).reshape(16, 8, R)


def sum_kernel(parts_ref, out_ref):
    out_ref[...] = jnp.sum(parts_ref[...].astype(f32), axis=0).astype(bf16)


def renew(own, parts):
    grad = jnp.sum(parts.astype(f32), axis=0)
    inverse = lax.rsqrt(jnp.sum(grad * grad, axis=1, keepdims=True) / R + epsilon)
    return own - step_size * grad * inverse


def renew_one_kernel(own_ref, parts_ref, out_ref):
    new = renew(own_ref[...], parts_ref[...]).astype(bf16)
    for b in range(8):
        out_ref[b] = new


def renew_two_kernel(own_ref, parts_ref, out_ref):
    new = renew(own_ref[...], parts_ref[...])
    for p in range(16):
        b = p % 4 * 4 + p // 4
        group = new[:, 128 * (b // 4) : 128 * (b // 4) + 128]
        turn = (128 - 32 * (b % 4)) % 128
        out_ref[p] = (pltpu.roll(group, turn, 1) if turn else group).astype(bf16)


def last_kernel(in_ref, out_ref):
    out_ref[...] = in_ref[...].reshape(128, 128).astype(f32).T[:32].astype(bf16)


VM = pl.BlockSpec(memory_space=pltpu.VMEM)
SM = pl.BlockSpec(memory_space=pltpu.SMEM)
HB = pl.BlockSpec(memory_space=pltpu.HBM)


def call(kernel, outs, specs, scratch=(), flops=0, nbytes=0, vmem=4):
    shapes = [jax.ShapeDtypeStruct(shape, dtype) for shape, dtype in outs]
    single = len(outs) == 1
    return pl.pallas_call(
        kernel,
        out_shape=shapes[0] if single else shapes,
        in_specs=specs,
        out_specs=VM if single else [VM] * len(outs),
        scratch_shapes=list(scratch),
        compiler_params=pltpu.CompilerParams(vmem_limit_bytes=vmem << 20),
        cost_estimate=pl.CostEstimate(flops=flops, bytes_accessed=nbytes, transcendentals=0),
    )


def groups():
    device = lambda n, yz, c: (n * 16 + yz) * 2 + c
    first = [[device(n, far_first(p), 1) for p in range(16)] for n in range(16)]
    second = [[device(p % 4 * 4 + p // 4, yz, 0) for p in range(16)] for yz in range(16)]
    return first + second


def pairs(first):
    return [[z % 4 * 2 + c, (z + 1) % 4 * 2 + 1 - c] for z in (first, first + 2) for c in range(2)]


def body(slices, mode_one, mode_two, slice_table, chosen):
    y, c = lax.axis_index("y"), lax.axis_index("c")
    odd = lax.axis_index("zh") & 1
    m, w = lax.axis_index(("x", "zl")), lax.axis_index(WIDE)
    pos = jnp.stack([((c ^ odd) * 4 + y) * 32, w * 16, m * 8, c, odd]).astype(jnp.int32)

    tiles = mode_one.T.reshape(2, 8, 2, 128).transpose(0, 2, 1, 3).reshape(4, 8, 128)
    blocks = jnp.concatenate([mode_two.T.reshape(4, 8, 128), tiles], axis=0)
    blocks = lax.all_gather(blocks, "c", axis=0).reshape(2, 2, 4, 8, 128)
    mine = lax.dynamic_index_in_dim(blocks, c, axis=1, keepdims=False)
    mine = jnp.broadcast_to(mine[None], (16, 2, 4, 8, 128))
    both = lax.all_to_all(mine, ALL, 0, 0, axis_index_groups=groups(), tiled=True)
    both = lax.all_gather(both, "c", axis=0)
    one_hot = (
        chosen[:, None] == lax.broadcasted_iota(jnp.int32, (chosen.shape[0], slice_table.shape[0]), 1)
    ).astype(bf16)
    slice_rows = jnp.dot(one_hot, slice_table, preferred_element_type=f32)
    t = call(fetch_kernel, [((BATCH, 256, 128), bf16)], [HB], (pltpu.SemaphoreType.DMA((CHUNKS,)),), nbytes=1 << 21)(slices)
    partial_one, own_one, two = call(
        first_kernel,
        [((8, 32, R), bf16), ((32, R), f32), ((128, R), f32)],
        [SM, VM, VM, VM],
        (pltpu.VMEM((R, 256), bf16), pltpu.VMEM((R, 128), bf16), pltpu.VMEM((256, R), bf16), pltpu.VMEM((128, R), f32), pltpu.VMEM((256, R), f32)),
        flops=1 << 31,
        vmem=16,
        nbytes=1 << 21,
    )(pos, slice_rows, both, t)
    parts = lax.all_to_all(partial_one, ("c", "y"), 0, 0, tiled=True)
    add = call(sum_kernel, [((32, R), bf16)], [VM])
    parts = lax.all_gather(add(parts), ("zh", "c"), axis=0, axis_index_groups=pairs(0))
    parts = lax.all_gather(add(parts), ("zh", "c"), axis=0, axis_index_groups=pairs(1))
    copies = call(renew_one_kernel, [((8, 32, R), bf16)], [VM, VM])(own_one, parts)
    new_full = lax.all_to_all(copies, ("c", "y"), 0, 0, tiled=True)

    partial_two, new_one_t, own_two = call(
        second_kernel,
        [((16, 8, R), bf16), ((16, 256), bf16), ((8, R), f32)],
        [SM, VM, VM, VM, VM],
        (pltpu.VMEM((256, R), bf16), pltpu.VMEM((128, R), f32)),
        flops=1 << 31,
        vmem=16,
        nbytes=1 << 21,
    )(pos, slice_rows, new_full, two, t)
    parts_two = lax.all_to_all(partial_two, ("x", "zl"), 0, 0, tiled=True)
    blocks = call(renew_two_kernel, [((16, 8, 128), bf16)], [VM, VM])(own_two, parts_two)
    blocks = lax.all_to_all(blocks, ("x", "zl"), 0, 0, tiled=True)
    new_two_t = call(last_kernel, [((32, 128), bf16)], [VM])(blocks)
    return (new_one_t.T, new_two_t.T)


def solution(mesh):
    fine = Mesh(mesh.devices.reshape(4, 4, 4, 4, 2), ("zl", "x", "y", "zh", "c"))
    in_specs = (P(None, NARROW, WIDE), P(NARROW, WIDE), P(WIDE, NARROW), P(), P())
    out_specs = (P(NARROW, WIDE), P(WIDE, NARROW))

    return jax.shard_map(body, mesh=fine, in_specs=in_specs, out_specs=out_specs, check_vma=False)
```
